32 devices in a mesh: grid: 16 (over z, y, x), col: 2 (over core).
Axes of the slice: x: 2, y: 2, z: 4, core: 2. Of those that a mesh axis runs over, the one named last changes fastest.
Arguments:
- orbitals: bfloat16 [884736, 256], P(('grid', 'col')), may hold values from -6 to 6
- points: int32 [1024], replicated, may hold values from 0 to 884735, as said below
- cinv: bfloat16 [1024, 256], replicated, may hold values from -0.1875 to 0.1875
Outputs:
- potential: bfloat16 [256, 884736], P(None, ('grid', 'col'))
- coupling: float32 [1024, 256], P(('grid', 'col'))
The draws below stay inside these ranges and needn't reach their ends.
Inputs may be any that keep to these rules, and one draw needn't show every extreme that they name: `points`: 1024 distinct grid rows.
All inputs are finite; a program needn't handle non-finite values.
Results may differ from the reference program's by a relative error of at most 0.0046.
Values may be sent and summed in bfloat16 or wider, within the bound.
No kernel may reach another device: no remote copies, remote signals or barrier semaphores. Data moves between devices by JAX's collectives and lax.ppermute only.
A program may use at most 448 MiB of HBM per device.

```python
import math
import jax
import jax.numpy as jnp
from jax import lax

NX = 96
NORB = 256
NMU = 1024
NCOL = 256
NGRID = 884736


def draw_points(key, part):
    order = jax.random.permutation(jax.random.fold_in(key, 7), NX ** 3)
    return order[:NMU].astype(jnp.int32)


def block_levels(stream_key, extent, split, least, high):
    factor_of, own = 1.0, jax.random.fold_in(stream_key, 6)
    for dim, shards_of in split:
        draws = jnp.exp(jax.random.uniform(jax.random.fold_in(own, dim), (shards_of,), jnp.float32, least / len(split), high / len(split)))
        factor_of = factor_of * jnp.repeat(draws, extent[dim] // shards_of).reshape([-1 if axis == dim else 1 for axis in range(len(extent))])
    return factor_of


def gaussian(stream_key, shape, width, reach, pieces=(), held_as=jnp.bfloat16):
    array = jax.random.normal(stream_key, shape, jnp.float32) * width
    if len(pieces) > 0:
        array = block_levels(stream_key, shape, pieces, -0.22, 0.18) * array
    return jnp.clip(array, min=-reach, max=reach).astype(held_as)


def setup_inputs(seed: int = 0) -> dict:
    seeds = jax.random.split(jax.random.key(seed), 4)
    return {
        "orbitals": gaussian(seeds[0], (NGRID, NORB), 1.0, 6.0, ((0, 32),)),
        "points": draw_points(jax.random.fold_in(seeds[3], 71), 0),
        "cinv": gaussian(seeds[2], (NMU, NCOL), NMU ** -0.5, 0.1875),
    }


screening = 0.25

def kernel_table(dtype):
    index = jnp.arange(NX)
    wave = jnp.where(index < (NX + 1) // 2, index, index - NX).astype(dtype) * (2.0 * math.pi / NX)
    squared = wave[:, None, None] ** 2 + wave[None, :, None] ** 2 + wave[None, None, :] ** 2
    return jnp.where(squared > 0, 1.0 / (squared + screening), 0.0).astype(dtype)

def reference(orbitals, points, cinv):
    point_rows = orbitals[points]
    scale = 1.0 / math.sqrt(NORB)

    def pair_of(block):
        product = jnp.dot(block, point_rows.T, preferred_element_type=jnp.float32) * scale
        return (product * product).astype(jnp.bfloat16)
    blocks = orbitals.reshape(NX, NX * NX, NORB)

    def fit(block):
        return jnp.dot(pair_of(block), cinv, preferred_element_type=jnp.float32)
    theta = lax.map(fit, blocks)
    fields = jnp.moveaxis(theta.reshape(NX, NX, NX, NCOL), 3, 0)
    table = kernel_table(theta.dtype)

    def solve(field):
        return jnp.fft.ifftn(table * jnp.fft.fftn(field)).real.astype(jnp.bfloat16)
    potential = lax.map(solve, fields).reshape(NCOL, NX ** 3)
    pot_blocks = jnp.moveaxis(potential.reshape(NCOL, NX, NX * NX), 1, 0)

    def accumulate(total, inputs):
        block, pots = inputs
        return (total + jnp.dot(pair_of(block).T, pots.T, preferred_element_type=jnp.float32), None)
    total, _ = lax.scan(accumulate, jnp.zeros((NMU, NCOL), jnp.float32), (blocks, pot_blocks))
    coupling = total * (math.sqrt(NMU) / NX ** 3)
    return (potential, coupling)
```

```python
import functools
import math

import jax
import jax.numpy as jnp
import numpy as np
from jax import lax
from jax.experimental import pallas as pl
from jax.experimental.pallas import tpu as pltpu
from jax.sharding import PartitionSpec as P

NX = 96


screening = 0.25


def kernel_table(size):
    index = jnp.arange(size)
    wave = jnp.where(index < (size + 1) // 2, index, index - size).astype(jnp.float32) * (
        2.0 * math.pi / size
    )
    squared = wave[:, None, None] ** 2 + wave[None, :, None] ** 2 + wave[None, None, :] ** 2
    return jnp.where(squared > 0, 1.0 / (squared + screening), 0.0)


def along(table, values, axis):
    forms = {1: "kn,cnyz->ckyz", 2: "kn,cxnz->cxkz", 3: "kn,cxyn->cxyk"}
    return jnp.einsum(forms[axis], table, values, precision=lax.Precision.HIGHEST)


def screened_solve(field):
    size = field.shape[1]
    index = jnp.arange(size, dtype=jnp.int32)
    phase = index[:, None] * index[None, :] % size
    angle = phase.astype(jnp.float32) * (2.0 * math.pi / size)
    cos_table = jnp.cos(angle)
    sin_table = jnp.sin(angle)
    real_part = along(cos_table, field, 3)
    imag_part = -along(sin_table, field, 3)
    for axis in (2, 1):
        real_part, imag_part = (
            along(cos_table, real_part, axis) + along(sin_table, imag_part, axis),
            along(cos_table, imag_part, axis) - along(sin_table, real_part, axis),
        )
    weights = kernel_table(size)
    real_part = real_part * weights
    imag_part = imag_part * weights
    for axis in (1, 2):
        real_part, imag_part = (
            along(cos_table, real_part, axis) - along(sin_table, imag_part, axis),
            along(cos_table, imag_part, axis) + along(sin_table, real_part, axis),
        )
    result = along(cos_table, real_part, 3) - along(sin_table, imag_part, 3)
    return result / float(size**3)


def local_columns(orbitals, points, cinv):
    ranks = lax.axis_size(("grid", "col"))
    local_rows = orbitals.shape[0]
    orbital_count = orbitals.shape[1]
    npoints = cinv.shape[0]
    columns = cinv.shape[1]
    per_rank = columns // ranks
    first_row = lax.axis_index(("grid", "col")) * local_rows
    offset = points - first_row
    inside = (offset >= 0) & (offset < local_rows)
    picked = jnp.take(orbitals, jnp.clip(offset, 0, local_rows - 1), axis=0)
    picked = jnp.where(inside[:, None], picked.astype(jnp.float32), 0.0)
    point_rows = lax.psum(picked, ("grid", "col")).astype(jnp.bfloat16)
    scale = 1.0 / math.sqrt(orbital_count)
    block_rows = math.gcd(local_rows, 1152)

    def pair_block(block):
        product = (
            lax.dot_general(
                block, point_rows, (((1,), (1,)), ((), ())), preferred_element_type=jnp.float32
            )
            * scale
        )
        return (product * product).astype(jnp.bfloat16)

    pairs = lax.map(
        pair_block, orbitals.reshape(local_rows // block_rows, block_rows, orbital_count)
    )
    pairs = pairs.reshape(local_rows, npoints)
    theta_cols = lax.dot_general(
        cinv, pairs, (((0,), (1,)), ((), ())), preferred_element_type=jnp.float32
    )
    fields = lax.all_to_all(theta_cols, ("grid", "col"), split_axis=0, concat_axis=1, tiled=True)
    fields = fields.reshape(per_rank, NX, NX, NX)
    potentials = screened_solve(fields).astype(jnp.bfloat16).reshape(per_rank, NX * NX * NX)
    rows_back = lax.all_to_all(potentials, ("grid", "col"), split_axis=1, concat_axis=0, tiled=True)
    factor = math.sqrt(npoints) / float(NX**3)
    halfway = lax.psum_scatter(
        lax.dot_general(
            pairs, rows_back, (((0,), (1,)), ((), ())), preferred_element_type=jnp.float32
        )
        * factor,
        "grid",
        scatter_dimension=0,
        tiled=True,
    )
    coupling = lax.psum_scatter(halfway, "col", scatter_dimension=0, tiled=True)
    return (rows_back, coupling)


AXES = ("grid", "col")
BF16, F32 = jnp.bfloat16, jnp.float32


def basis(size):
    wave = np.arange(size)[:, None]
    cell = np.arange(size)[None, :]
    angle = 2.0 * np.pi * (wave * cell % size) / size
    rows = np.where(2 * wave <= size, np.cos(angle), np.sin(angle)) * np.sqrt(2.0 / size)
    rows[0] = np.sqrt(1.0 / size)
    if size % 2 == 0:
        rows[size // 2] *= np.sqrt(0.5)
    number = np.minimum(np.arange(size), size - np.arange(size))
    return rows, (number * (2.0 * np.pi / size)) ** 2


def split_table(table):
    high = np.asarray(table, BF16)
    low = np.asarray(table - high.astype(np.float64), BF16)
    return np.concatenate([high, low], axis=0)


def dot(left, right):
    return lax.dot_general(left, right, (((1,), (0,)), ((), ())), preferred_element_type=F32)


def apply_exact(table, values):
    both = dot(table, values)
    half = table.shape[0] // 2
    return both[:half] + both[half:]


def apply_split(table, values):
    high = values.astype(BF16)
    low = (values - high.astype(F32)).astype(BF16)
    half = table.shape[0] // 2
    return apply_exact(table, high) + dot(table[:half], low)


LANES = 128


def strided_load(ref, start, count, stride):
    parts = [
        ref[half, pl.ds(start, count, stride=stride), :] for half in range(ref.shape[0])
    ]
    return jnp.concatenate(parts, axis=1)


def strided_store(ref, start, count, stride, value):
    for half in range(ref.shape[0]):
        ref[half, pl.ds(start, count, stride=stride), :] = value[:, half * LANES : (half + 1) * LANES]


def load(ref, start, count):
    parts = [ref[half, pl.ds(start, count), :] for half in range(ref.shape[0])]
    return jnp.concatenate(parts, axis=1)


def store(ref, start, count, value):
    for half in range(ref.shape[0]):
        ref[half, pl.ds(start, count), :] = value[:, half * LANES : (half + 1) * LANES]


def fit_kernel(size, scale, orb_ref, pts_ref, cinv_ref, table_ref, pair_ref, *rest):
    outs, (field, points, shift) = rest[:-3], rest[-3:]
    step = pl.program_id(0)
    rows = orb_ref.shape[0]
    npoints = pts_ref.shape[0]
    thirds = len(outs)
    table = table_ref[...]

    @pl.when(step == 0)
    def _():
        scaled = pts_ref[...].astype(F32) * scale
        points[...] = scaled.astype(BF16)
        square = scaled * scaled
        norm = jnp.sum(square, axis=1, keepdims=True)
        mean = norm * (jnp.sum(norm) / npoints)
        shift[...] = jnp.sum(mean * cinv_ref[...].astype(F32), axis=0, keepdims=True)

    product = lax.dot_general(
        orb_ref[...], points[...], (((1,), (1,)), ((), ())), preferred_element_type=F32
    )
    pair = (product * product).astype(BF16)
    pair_ref[...] = pair
    theta = dot(pair, cinv_ref[...]) - shift[...]
    for line in range(rows // size):
        value = apply_split(table, theta[line * size : (line + 1) * size])
        store(field, pl.multiple_of(step * rows + line * size, size), size, value)

    @pl.when(step == pl.num_programs(0) - 1)
    def _():
        def body(owner, carry):
            for third in range(thirds):
                value = strided_load(field, owner * thirds + third, size, size)
                value = apply_split(table, value)
                outs[third][pl.ds(pl.multiple_of(owner * size, size), size), :] = value.astype(BF16)
            return carry

        lax.fori_loop(0, size // thirds, body, 0)


def solve_kernel(size, wave_b_ref, wave_c_ref, wave_a_ref, table_ref, back_ref, *rest):
    planes = (len(rest) - 1) // 2
    ins, outs, field = rest[:planes], rest[planes : 2 * planes], rest[-1]
    owners = size // planes
    for plane in range(planes):
        def widen(owner, carry):
            start = pl.multiple_of(owner * size, size)
            store(
                field,
                pl.multiple_of(plane * owners * size + start, size),
                size,
                ins[plane][pl.ds(start, size), :].astype(F32),
            )
            return carry

        lax.fori_loop(0, owners, widen, 0)
    table, back = table_ref[...], back_ref[...]
    wave_a = wave_a_ref[...]

    def body(mode, carry):
        value = jnp.concatenate(
            [
                strided_load(field, plane * owners * size + mode, owners, size)
                for plane in range(planes)
            ],
            axis=0,
        )
        value = apply_exact(table, value.astype(BF16))
        squared = wave_a + (wave_b_ref[mode] + wave_c_ref[0])
        weight = jnp.where(squared > 0, 1.0 / (squared + screening), 0.0)
        value = apply_split(back, value * weight)
        for plane in range(planes):
            strided_store(
                field,
                plane * owners * size + mode,
                owners,
                size,
                value[plane * owners : (plane + 1) * owners],
            )
        return carry

    lax.fori_loop(0, size, body, 0)
    for plane in range(planes):
        def narrow(owner, carry):
            start = pl.multiple_of(owner * size, size)
            value = load(field, pl.multiple_of(plane * owners * size + start, size), size)
            outs[plane][pl.ds(start, size), :] = value.astype(BF16)
            return carry

        lax.fori_loop(0, owners, narrow, 0)


def couple_kernel(size, thirds, first, last, factor, *rest):
    ins = rest[:thirds]
    table_ref, pair_ref = rest[thirds : thirds + 2]
    rest = rest[thirds + 2 :]
    if not first:
        before_ref, rest = rest[0], rest[2:]
    out_ref, total_ref, field, block, total = rest
    step = pl.program_id(0)
    table = table_ref[...]
    rows = pair_ref.shape[0]

    @pl.when(step == 0)
    def _():
        if first:
            total[...] = jnp.zeros_like(total)
        else:
            total[...] = before_ref[...]

        def body(owner, carry):
            for third in range(thirds):
                value = ins[third][pl.ds(pl.multiple_of(owner * size, size), size), :]
                value = apply_exact(table, value)
                strided_store(field, owner * thirds + third, size, size, value)
            return carry

        lax.fori_loop(0, size // thirds, body, 0)

    for line in range(rows // size):
        value = load(field, pl.multiple_of(step * rows + line * size, size), size)
        block[line * size : (line + 1) * size, :] = apply_split(table, value)
    turned = block[...].T.astype(BF16)
    out_ref[...] = turned
    total[...] += dot(turned, pair_ref[...])

    @pl.when(step == pl.num_programs(0) - 1)
    def _():
        if last:
            total_ref[...] = total[...].T * factor
        else:
            total_ref[...] = total[...]


def const_spec(shape):
    return pl.BlockSpec(shape, lambda *_: (0,) * len(shape))


def cost(flops, moved):
    return pl.CostEstimate(flops=int(flops), bytes_accessed=int(moved), transcendentals=0)


VMEM = 60000 * 1024


def local_planes(orbitals, points, cinv):
    size = NX
    ranks = lax.axis_size(AXES)
    rank = lax.axis_index(AXES)
    local_rows, orbital_count = orbitals.shape
    npoints, columns = cinv.shape
    plane_rows = size * size
    planes = local_rows // plane_rows
    halves = columns // LANES

    offset = points - rank * local_rows
    inside = (offset >= 0) & (offset < local_rows)
    picked = jnp.take(orbitals, jnp.clip(offset, 0, local_rows - 1), axis=0)
    picked = jnp.where(inside[:, None], picked, jnp.zeros_like(picked))
    point_rows = lax.psum(picked, AXES)

    rows, squared = basis(size)
    forward = jnp.asarray(split_table(rows))
    inverse = jnp.asarray(split_table(rows.T))
    order = (np.arange(ranks)[None, :] * planes + np.arange(planes)[:, None]).reshape(-1)
    forward_a = jnp.asarray(split_table(rows[:, order]))
    inverse_a = jnp.asarray(split_table(rows.T[order]))
    wave = jnp.asarray(squared, F32)
    wave_a = jnp.asarray(np.broadcast_to(squared[:, None], (size, columns)), F32)

    lines = 8
    while size % lines:
        lines -= 1
    block_rows = lines * size
    steps = size // lines
    scale = 1.0 / math.sqrt(orbital_count)
    spectrum = jax.ShapeDtypeStruct((ranks * size, columns), BF16)
    transform = 2 * 3 * plane_rows * size * columns

    pairs, sent = [], []
    for plane in range(planes):
        result = pl.pallas_call(
            functools.partial(fit_kernel, size, scale),
            grid=(steps,),
            in_specs=[
                pl.BlockSpec((block_rows, orbital_count), lambda i, plane=plane: (plane * steps + i, 0)),
                const_spec((npoints, orbital_count)),
                const_spec((npoints, columns)),
                const_spec(forward.shape),
            ],
            out_specs=[pl.BlockSpec((block_rows, npoints), lambda i: (i, 0))]
            + [const_spec(spectrum.shape)] * planes,
            out_shape=[jax.ShapeDtypeStruct((plane_rows, npoints), BF16)] + [spectrum] * planes,
            scratch_shapes=[
                pltpu.VMEM((halves, plane_rows, LANES), F32),
                pltpu.VMEM((npoints, orbital_count), BF16),
                pltpu.VMEM((1, columns), F32),
            ],
            compiler_params=pltpu.CompilerParams(
                dimension_semantics=("arbitrary",), vmem_limit_bytes=VMEM
            ),
            cost_estimate=cost(
                2 * plane_rows * npoints * (orbital_count + columns) + 2 * transform,
                plane_rows * (2 * orbital_count + 2 * npoints + 2 * columns),
            ),
            name="fit",
        )(orbitals, point_rows, cinv, forward)
        pairs.append(result[0])
        sent.append(result[1:])

    def exchange(array):
        shaped = array.reshape(ranks, size, columns)
        return lax.all_to_all(shaped, AXES, 0, 0, tiled=True).reshape(array.shape)

    solved = []
    for third in range(planes):
        arrived = [exchange(sent[plane][third]) for plane in range(planes)]
        wave_c = lax.dynamic_slice(wave, (rank * planes + third,), (1,))
        smem = pl.BlockSpec(memory_space=pltpu.SMEM)
        solved.append(
            pl.pallas_call(
                functools.partial(solve_kernel, size),
                in_specs=[smem, smem] + [pl.BlockSpec(memory_space=pltpu.VMEM)] * (3 + planes),
                out_specs=[pl.BlockSpec(memory_space=pltpu.VMEM)] * planes,
                out_shape=[spectrum] * planes,
                scratch_shapes=[pltpu.VMEM((halves, plane_rows, LANES), F32)],
                compiler_params=pltpu.CompilerParams(vmem_limit_bytes=VMEM),
                cost_estimate=cost(2 * transform, 4 * plane_rows * columns),
                name="solve",
            )(wave, wave_c, wave_a, forward_a, inverse_a, *arrived)
        )

    factor = math.sqrt(npoints) / float(size**3)
    potential = total = None
    returned = [[exchange(solved[third][plane]) for third in range(planes)] for plane in range(planes)]
    for plane in range(planes):
        first, last = plane == 0, plane == planes - 1
        in_specs = [const_spec(spectrum.shape)] * planes + [
            const_spec(inverse.shape),
            pl.BlockSpec((block_rows, npoints), lambda i: (i, 0)),
        ]
        operands = [*returned[plane], inverse, pairs[plane]]
        if not first:
            in_specs += [const_spec(total.shape), pl.BlockSpec(memory_space=pl.ANY)]
            operands += [total, potential]
        total_shape = (npoints, columns) if last else (columns, npoints)
        potential, total = pl.pallas_call(
            functools.partial(couple_kernel, size, planes, first, last, factor),
            grid=(steps,),
            in_specs=in_specs,
            out_specs=[
                pl.BlockSpec((columns, block_rows), lambda i, plane=plane: (0, plane * steps + i)),
                const_spec(total_shape),
            ],
            out_shape=[
                jax.ShapeDtypeStruct((columns, local_rows), BF16),
                jax.ShapeDtypeStruct(total_shape, F32),
            ],
            scratch_shapes=[
                pltpu.VMEM((halves, plane_rows, LANES), F32),
                pltpu.VMEM((block_rows, columns), F32),
                pltpu.VMEM((columns, npoints), F32),
            ],
            input_output_aliases={} if first else {len(operands) - 1: 0},
            compiler_params=pltpu.CompilerParams(
                dimension_semantics=("arbitrary",), vmem_limit_bytes=VMEM
            ),
            cost_estimate=cost(
                2 * plane_rows * npoints * columns + 2 * transform,
                plane_rows * (2 * npoints + 4 * columns),
            ),
            name="couple",
        )(*operands)

    shares = lax.all_to_all(
        total.reshape(ranks, npoints // ranks, columns), AXES, 0, 0, tiled=True
    )
    return potential, jnp.sum(shares, axis=0)


def local(orbitals, points, cinv):
    size = NX
    ranks = lax.axis_size(AXES)
    rows, orbital_count = orbitals.shape
    npoints, columns = cinv.shape
    whole = rows * ranks == size**3 and rows % (size * size) == 0 and size % 16 == 0
    exact = math.frexp(1.0 / math.sqrt(orbital_count))[0] == 0.5
    if whole and exact and columns % LANES == 0 and npoints % (ranks * 8) == 0:
        return local_planes(orbitals, points, cinv)
    return local_columns(orbitals, points, cinv)


def solution(mesh):
    in_specs = (P(("grid", "col"), None), P(), P())
    out_specs = (P(None, ("grid", "col")), P(("grid", "col"), None))
    return jax.shard_map(local, mesh=mesh, in_specs=in_specs, out_specs=out_specs, check_vma=False)
```

```python
import functools
import math

import jax
import jax.numpy as jnp
import numpy as np
from jax import lax
from jax.experimental import pallas as pl
from jax.experimental.pallas import tpu as pltpu
from jax.sharding import PartitionSpec as P

NX = 96


screening = 0.25


def kernel_table(size):
    index = jnp.arange(size)
    wave = jnp.where(index < (size + 1) // 2, index, index - size).astype(jnp.float32) * (
        2.0 * math.pi / size
    )
    squared = wave[:, None, None] ** 2 + wave[None, :, None] ** 2 + wave[None, None, :] ** 2
    return jnp.where(squared > 0, 1.0 / (squared + screening), 0.0)


def along(table, values, axis):
    forms = {1: "kn,cnyz->ckyz", 2: "kn,cxnz->cxkz", 3: "kn,cxyn->cxyk"}
    return jnp.einsum(forms[axis], table, values, precision=lax.Precision.HIGHEST)


def screened_solve(field):
    size = field.shape[1]
    index = jnp.arange(size, dtype=jnp.int32)
    phase = index[:, None] * index[None, :] % size
    angle = phase.astype(jnp.float32) * (2.0 * math.pi / size)
    cos_table = jnp.cos(angle)
    sin_table = jnp.sin(angle)
    real_part = along(cos_table, field, 3)
    imag_part = -along(sin_table, field, 3)
    for axis in (2, 1):
        real_part, imag_part = (
            along(cos_table, real_part, axis) + along(sin_table, imag_part, axis),
            along(cos_table, imag_part, axis) - along(sin_table, real_part, axis),
        )
    weights = kernel_table(size)
    real_part = real_part * weights
    imag_part = imag_part * weights
    for axis in (1, 2):
        real_part, imag_part = (
            along(cos_table, real_part, axis) - along(sin_table, imag_part, axis),
            along(cos_table, imag_part, axis) + along(sin_table, real_part, axis),
        )
    result = along(cos_table, real_part, 3) - along(sin_table, imag_part, 3)
    return result / float(size**3)


def local_columns(orbitals, points, cinv):
    ranks = lax.axis_size(("grid", "col"))
    local_rows = orbitals.shape[0]
    orbital_count = orbitals.shape[1]
    npoints = cinv.shape[0]
    columns = cinv.shape[1]
    per_rank = columns // ranks
    first_row = lax.axis_index(("grid", "col")) * local_rows
    offset = points - first_row
    inside = (offset >= 0) & (offset < local_rows)
    picked = jnp.take(orbitals, jnp.clip(offset, 0, local_rows - 1), axis=0)
    picked = jnp.where(inside[:, None], picked.astype(jnp.float32), 0.0)
    point_rows = lax.psum(picked, ("grid", "col")).astype(jnp.bfloat16)
    scale = 1.0 / math.sqrt(orbital_count)
    block_rows = math.gcd(local_rows, 1152)

    def pair_block(block):
        product = (
            lax.dot_general(
                block, point_rows, (((1,), (1,)), ((), ())), preferred_element_type=jnp.float32
            )
            * scale
        )
        return (product * product).astype(jnp.bfloat16)

    pairs = lax.map(
        pair_block, orbitals.reshape(local_rows // block_rows, block_rows, orbital_count)
    )
    pairs = pairs.reshape(local_rows, npoints)
    theta_cols = lax.dot_general(
        cinv, pairs, (((0,), (1,)), ((), ())), preferred_element_type=jnp.float32
    )
    fields = lax.all_to_all(theta_cols, ("grid", "col"), split_axis=0, concat_axis=1, tiled=True)
    fields = fields.reshape(per_rank, NX, NX, NX)
    potentials = screened_solve(fields).astype(jnp.bfloat16).reshape(per_rank, NX * NX * NX)
    rows_back = lax.all_to_all(potentials, ("grid", "col"), split_axis=1, concat_axis=0, tiled=True)
    factor = math.sqrt(npoints) / float(NX**3)
    halfway = lax.psum_scatter(
        lax.dot_general(
            pairs, rows_back, (((0,), (1,)), ((), ())), preferred_element_type=jnp.float32
        )
        * factor,
        "grid",
        scatter_dimension=0,
        tiled=True,
    )
    coupling = lax.psum_scatter(halfway, "col", scatter_dimension=0, tiled=True)
    return (rows_back, coupling)


AXES = ("grid", "col")
BF16, F32 = jnp.bfloat16, jnp.float32


def basis(size):
    wave = np.arange(size)[:, None]
    cell = np.arange(size)[None, :]
    angle = 2.0 * np.pi * (wave * cell % size) / size
    rows = np.where(2 * wave <= size, np.cos(angle), np.sin(angle)) * np.sqrt(2.0 / size)
    rows[0] = np.sqrt(1.0 / size)
    if size % 2 == 0:
        rows[size // 2] *= np.sqrt(0.5)
    number = np.minimum(np.arange(size), size - np.arange(size))
    return rows, (number * (2.0 * np.pi / size)) ** 2


def split_table(table):
    high = np.asarray(table, BF16)
    low = np.asarray(table - high.astype(np.float64), BF16)
    return np.concatenate([high, low], axis=0)


def dot(left, right):
    return lax.dot_general(left, right, (((1,), (0,)), ((), ())), preferred_element_type=F32)


def apply_exact(table, values):
    both = dot(table, values)
    half = table.shape[0] // 2
    return both[:half] + both[half:]


def apply_split(table, values):
    high = values.astype(BF16)
    low = (values - high.astype(F32)).astype(BF16)
    half = table.shape[0] // 2
    return apply_exact(table, high) + dot(table[:half], low)


LANES = 128


def strided_load(ref, start, count, stride):
    parts = [
        ref[half, pl.ds(start, count, stride=stride), :] for half in range(ref.shape[0])
    ]
    return jnp.concatenate(parts, axis=1)


def strided_store(ref, start, count, stride, value):
    for half in range(ref.shape[0]):
        ref[half, pl.ds(start, count, stride=stride), :] = value[:, half * LANES : (half + 1) * LANES]


def load(ref, start, count):
    parts = [ref[half, pl.ds(start, count), :] for half in range(ref.shape[0])]
    return jnp.concatenate(parts, axis=1)


def store(ref, start, count, value):
    for half in range(ref.shape[0]):
        ref[half, pl.ds(start, count), :] = value[:, half * LANES : (half + 1) * LANES]


def fit_kernel(size, scale, single, orb_ref, pts_ref, cinv_ref, table_ref, *rest):
    if not single:
        rest = rest[1:]
    pair_ref, outs, (field, points, shift) = rest[0], rest[1:-3], rest[-3:]
    plane, step = pl.program_id(0), pl.program_id(1)
    rows = orb_ref.shape[0]
    npoints = pts_ref.shape[0]
    thirds = outs[0].shape[1] if single else len(outs)
    table = table_ref[...]

    @pl.when((plane == 0) & (step == 0))
    def _():
        scaled = pts_ref[...].astype(F32) * scale
        points[...] = scaled.astype(BF16)
        square = scaled * scaled
        norm = jnp.sum(square, axis=1, keepdims=True)
        mean = norm * (jnp.sum(norm) / npoints)
        shift[...] = jnp.sum(mean * cinv_ref[...].astype(F32), axis=0, keepdims=True)

    product = lax.dot_general(
        orb_ref[...], points[...], (((1,), (1,)), ((), ())), preferred_element_type=F32
    )
    pair = (product * product).astype(BF16)
    pair_ref[...] = pair
    theta = dot(pair, cinv_ref[...]) - shift[...]
    for line in range(rows // size):
        value = apply_split(table, theta[line * size : (line + 1) * size])
        store(field, pl.multiple_of(step * rows + line * size, size), size, value)

    @pl.when(step == pl.num_programs(1) - 1)
    def _():
        def body(owner, carry):
            for third in range(thirds):
                value = strided_load(field, owner * thirds + third, size, size)
                value = apply_split(table, value).astype(BF16)
                if single:
                    outs[0][owner, third] = value
                else:
                    outs[third][owner, plane] = value
            return carry

        lax.fori_loop(0, size // thirds, body, 0)


def solve_kernel(size, passed, wave_b_ref, wave_c_ref, wave_a_ref, table_ref, back_ref, *rest):
    first_ref, rest_ref = rest[:2]
    outs, field = rest[2 + passed : -1], rest[-1]
    owners, later = rest_ref.shape[:2]
    planes = later + 1
    plane_rows = owners * size

    def widen(owner, carry):
        for plane in range(planes):
            value = first_ref[owner, 0] if plane == 0 else rest_ref[owner, plane - 1]
            start = pl.multiple_of(plane * plane_rows + owner * size, size)
            store(field, start, size, value.astype(F32))
        return carry

    lax.fori_loop(0, owners, widen, 0)
    table, back = table_ref[...], back_ref[...]
    wave_a = wave_a_ref[...]

    def body(mode, carry):
        value = jnp.concatenate(
            [strided_load(field, p * plane_rows + mode, owners, size) for p in range(planes)],
            axis=0,
        )
        value = apply_exact(table, value.astype(BF16))
        squared = wave_a + (wave_b_ref[mode] + wave_c_ref[0])
        weight = jnp.where(squared > 0, 1.0 / (squared + screening), 0.0)
        value = apply_split(back, value * weight)
        for p in range(planes):
            part = value[p * owners : (p + 1) * owners]
            strided_store(field, p * plane_rows + mode, owners, size, part)
        return carry

    lax.fori_loop(0, size, body, 0)

    def narrow(owner, carry):
        for plane in range(planes):
            start = pl.multiple_of(plane * plane_rows + owner * size, size)
            value = load(field, start, size).astype(BF16)
            if len(outs) == 1:
                outs[0][owner, plane] = value
            elif plane < later:
                outs[0][owner, 0, plane] = value
            else:
                outs[1][owner, 0] = value
        return carry

    lax.fori_loop(0, owners, narrow, 0)


def couple_kernel(size, first, last, factor, *rest):
    first_ref, rest_ref, table_ref, pair_ref = rest[:4]
    rest = rest[4:]
    if not first:
        before_ref, rest = rest[0], rest[2:]
    out_ref, total_ref, field, block, total = rest
    step = pl.program_id(0)
    table = table_ref[...]
    rows = pair_ref.shape[0]
    owners, later = rest_ref.shape[:2]

    @pl.when(step == 0)
    def _():
        if first:
            total[...] = jnp.zeros_like(total)
        else:
            total[...] = before_ref[...]

        def body(owner, carry):
            for third in range(later + 1):
                if third == 0:
                    value = first_ref[owner, 0]
                elif last:
                    value = rest_ref[owner, third - 1]
                else:
                    value = rest_ref[owner, third - 1, 0]
                value = apply_exact(table, value)
                strided_store(field, owner * (later + 1) + third, size, size, value)
            return carry

        lax.fori_loop(0, owners, body, 0)

    for line in range(rows // size):
        value = load(field, pl.multiple_of(step * rows + line * size, size), size)
        block[line * size : (line + 1) * size, :] = apply_split(table, value)
    turned = block[...].T.astype(BF16)
    out_ref[...] = turned
    total[...] += dot(turned, pair_ref[...])

    @pl.when(step == pl.num_programs(0) - 1)
    def _():
        if last:
            total_ref[...] = total[...].T * factor
        else:
            total_ref[...] = total[...]


def const_spec(shape):
    return pl.BlockSpec(shape, lambda *_: (0,) * len(shape))


def cost(flops, moved):
    return pl.CostEstimate(flops=int(flops), bytes_accessed=int(moved), transcendentals=0)


VMEM = 60000 * 1024


def local_planes(orbitals, points, cinv):
    size = NX
    ranks = lax.axis_size(AXES)
    rank = lax.axis_index(AXES)
    local_rows, orbital_count = orbitals.shape
    npoints, columns = cinv.shape
    plane_rows = size * size
    planes = local_rows // plane_rows
    later = planes - 1
    halves = columns // LANES

    arrivals = []

    def exchange(array, *after):
        if arrivals:
            array, *_ = lax.optimization_barrier((array, arrivals[-1], *after))
        arrivals.append(lax.all_to_all(array, AXES, 0, 0, tiled=True))
        return arrivals[-1]

    offset = points - rank * local_rows
    inside = (offset >= 0) & (offset < local_rows)
    picked = jnp.take(orbitals, jnp.clip(offset, 0, local_rows - 1), axis=0)
    picked = jnp.where(inside[:, None], picked, jnp.zeros_like(picked))
    shares = exchange(picked.reshape(ranks, npoints // ranks, orbital_count))
    share = jnp.sum(shares.astype(F32), axis=0).astype(BF16)
    point_rows = exchange(jnp.broadcast_to(share[None], shares.shape))
    point_rows = point_rows.reshape(npoints, orbital_count)

    rows, squared = basis(size)
    forward = jnp.asarray(split_table(rows))
    inverse = jnp.asarray(split_table(rows.T))
    order = (np.arange(ranks)[None, :] * planes + np.arange(planes)[:, None]).reshape(-1)
    forward_a = jnp.asarray(split_table(rows[:, order]))
    inverse_a = jnp.asarray(split_table(rows.T[order]))
    wave = jnp.asarray(squared, F32)
    wave_a = jnp.asarray(np.broadcast_to(squared[:, None], (size, columns)), F32)

    lines = 8
    while size % lines:
        lines -= 1
    block_rows = lines * size
    steps = size // lines
    scale = 1.0 / math.sqrt(orbital_count)
    transform = 2 * 3 * plane_rows * size * columns
    tile = (size, columns)

    smem = pl.BlockSpec(memory_space=pltpu.SMEM)
    anywhere = pl.BlockSpec(memory_space=pl.ANY)

    def fit(start, count, *after):
        shape = (ranks, planes if count == 1 else count, *tile)
        outs = 1 if count == 1 else planes
        pair, *sent = pl.pallas_call(
            functools.partial(fit_kernel, size, scale, count == 1),
            grid=(count, steps),
            in_specs=[
                pl.BlockSpec((block_rows, orbital_count), lambda p, i: ((start + p) * steps + i, 0)),
                const_spec((npoints, orbital_count)),
                const_spec((npoints, columns)),
                const_spec(forward.shape),
            ]
            + [anywhere] * len(after),
            out_specs=[pl.BlockSpec((block_rows, npoints), lambda p, i: (p * steps + i, 0))]
            + [const_spec(shape)] * outs,
            out_shape=[jax.ShapeDtypeStruct((count * plane_rows, npoints), BF16)]
            + [jax.ShapeDtypeStruct(shape, BF16)] * outs,
            scratch_shapes=[
                pltpu.VMEM((halves, plane_rows, LANES), F32),
                pltpu.VMEM((npoints, orbital_count), BF16),
                pltpu.VMEM((1, columns), F32),
            ],
            compiler_params=pltpu.CompilerParams(
                dimension_semantics=("arbitrary", "arbitrary"), vmem_limit_bytes=VMEM
            ),
            cost_estimate=cost(
                count * (2 * plane_rows * npoints * (orbital_count + columns) + 2 * transform),
                count * plane_rows * (2 * orbital_count + 2 * npoints + 2 * columns),
            ),
            name="fit",
        )(orbitals, point_rows, cinv, forward, *after)
        return pair, sent

    pair_first, (sent_first,) = fit(0, 1)
    arrived_first = exchange(sent_first)
    pair_rest, sent_rest = fit(1, later, pair_first)

    arrived_rest = [exchange(value) for value in sent_rest[:2]]
    back_first = back_rest = arrived_back = None
    for third in range(planes):
        if third > 0 and third + 1 < planes:
            arrived_rest.append(exchange(sent_rest[third + 1], back_first if third == 1 else back_rest[0]))
        arrived = arrived_rest[third]
        wave_c = lax.dynamic_slice(wave, (rank * planes + third,), (1,))
        operands = [wave, wave_c, wave_a, forward_a, inverse_a, arrived_first, arrived]
        in_specs = [smem, smem] + [const_spec(value.shape) for value in operands[2:5]]
        in_specs += [
            pl.BlockSpec((ranks, 1, *tile), lambda i, third=third: (0, third, 0, 0)),
            const_spec((ranks, later, *tile)),
        ]
        passed, aliases = 0, {}
        if third == 0:
            shapes = [(ranks, planes, *tile)]
            out_specs = [const_spec(shapes[0])]
        else:
            shapes = [(ranks, later, later, *tile), (ranks, later, *tile)]
            out_specs = [
                pl.BlockSpec((ranks, 1, later, *tile), lambda i, third=third: (0, third - 1, 0, 0, 0)),
                pl.BlockSpec((ranks, 1, *tile), lambda i, third=third: (0, third - 1, 0, 0)),
            ]
            if third > 1:
                passed = len(back_rest)
                aliases = {len(operands) + k: k for k in range(passed)}
                operands += back_rest
                in_specs += [anywhere] * passed
        result = pl.pallas_call(
            functools.partial(solve_kernel, size, passed),
            grid=(1,),
            in_specs=in_specs,
            out_specs=out_specs,
            out_shape=[jax.ShapeDtypeStruct(shape, BF16) for shape in shapes],
            scratch_shapes=[pltpu.VMEM((halves, plane_rows, LANES), F32)],
            input_output_aliases=aliases,
            compiler_params=pltpu.CompilerParams(vmem_limit_bytes=VMEM),
            cost_estimate=cost(2 * transform, 4 * plane_rows * columns),
            name="solve",
        )(*operands)
        if third == 0:
            back_first = result[0]
        else:
            back_rest = result
        if third == max(planes - 2, 0):
            arrived_back = exchange(back_first, result[0])

    back_first = arrived_back
    back_rest = [exchange(value) for value in back_rest]

    factor = math.sqrt(npoints) / float(size**3)
    potential = total = None
    for plane in range(planes):
        first, last = plane == 0, plane == planes - 1
        pair_start = 0 if first else (plane - 1) * steps
        if last:
            rest_spec = const_spec((ranks, later, *tile))
        else:
            rest_spec = pl.BlockSpec(
                (ranks, later, 1, *tile), lambda i, plane=plane: (0, 0, plane, 0, 0)
            )
        in_specs = [
            pl.BlockSpec((ranks, 1, *tile), lambda i, plane=plane: (0, plane, 0, 0)),
            rest_spec,
            const_spec(inverse.shape),
            pl.BlockSpec((block_rows, npoints), lambda i, start=pair_start: (start + i, 0)),
        ]
        operands = [back_first, back_rest[last], inverse, pair_first if first else pair_rest]
        if not first:
            in_specs += [const_spec(total.shape), anywhere]
            operands += [total, potential]
        total_shape = (npoints, columns) if last else (columns, npoints)
        potential, total = pl.pallas_call(
            functools.partial(couple_kernel, size, first, last, factor),
            grid=(steps,),
            in_specs=in_specs,
            out_specs=[
                pl.BlockSpec((columns, block_rows), lambda i, plane=plane: (0, plane * steps + i)),
                const_spec(total_shape),
            ],
            out_shape=[
                jax.ShapeDtypeStruct((columns, local_rows), BF16),
                jax.ShapeDtypeStruct(total_shape, F32),
            ],
            scratch_shapes=[
                pltpu.VMEM((halves, plane_rows, LANES), F32),
                pltpu.VMEM((block_rows, columns), F32),
                pltpu.VMEM((columns, npoints), F32),
            ],
            input_output_aliases={} if first else {len(operands) - 1: 0},
            compiler_params=pltpu.CompilerParams(
                dimension_semantics=("arbitrary",), vmem_limit_bytes=VMEM
            ),
            cost_estimate=cost(
                2 * plane_rows * npoints * columns + 2 * transform,
                plane_rows * (2 * npoints + 4 * columns),
            ),
            name="couple",
        )(*operands)

    shares = exchange(total.reshape(ranks, npoints // ranks, columns))
    return potential, jnp.sum(shares, axis=0)


def local(orbitals, points, cinv):
    size = NX
    ranks = lax.axis_size(AXES)
    rows, orbital_count = orbitals.shape
    npoints, columns = cinv.shape
    whole = rows * ranks == size**3 and rows % (size * size) == 0 and size % 16 == 0
    whole = whole and rows >= 2 * size * size
    exact = math.frexp(1.0 / math.sqrt(orbital_count))[0] == 0.5
    if whole and exact and columns % LANES == 0 and npoints % (ranks * 8) == 0:
        return local_planes(orbitals, points, cinv)
    return local_columns(orbitals, points, cinv)


def solution(mesh):
    in_specs = (P(("grid", "col"), None), P(), P())
    out_specs = (P(None, ("grid", "col")), P(("grid", "col"), None))
    return jax.shard_map(local, mesh=mesh, in_specs=in_specs, out_specs=out_specs, check_vma=False)
```

```python
import functools
import math

import jax
import jax.numpy as jnp
import numpy as np
from jax import lax
from jax.experimental import pallas as pl
from jax.experimental.pallas import tpu as pltpu
from jax.sharding import PartitionSpec as P

NX = 96


screening = 0.25


def kernel_table(size):
    index = jnp.arange(size)
    wave = jnp.where(index < (size + 1) // 2, index, index - size).astype(jnp.float32) * (
        2.0 * math.pi / size
    )
    squared = wave[:, None, None] ** 2 + wave[None, :, None] ** 2 + wave[None, None, :] ** 2
    return jnp.where(squared > 0, 1.0 / (squared + screening), 0.0)


def along(table, values, axis):
    forms = {1: "kn,cnyz->ckyz", 2: "kn,cxnz->cxkz", 3: "kn,cxyn->cxyk"}
    return jnp.einsum(forms[axis], table, values, precision=lax.Precision.HIGHEST)


def screened_solve(field):
    size = field.shape[1]
    index = jnp.arange(size, dtype=jnp.int32)
    phase = index[:, None] * index[None, :] % size
    angle = phase.astype(jnp.float32) * (2.0 * math.pi / size)
    cos_table = jnp.cos(angle)
    sin_table = jnp.sin(angle)
    real_part = along(cos_table, field, 3)
    imag_part = -along(sin_table, field, 3)
    for axis in (2, 1):
        real_part, imag_part = (
            along(cos_table, real_part, axis) + along(sin_table, imag_part, axis),
            along(cos_table, imag_part, axis) - along(sin_table, real_part, axis),
        )
    weights = kernel_table(size)
    real_part = real_part * weights
    imag_part = imag_part * weights
    for axis in (1, 2):
        real_part, imag_part = (
            along(cos_table, real_part, axis) - along(sin_table, imag_part, axis),
            along(cos_table, imag_part, axis) + along(sin_table, real_part, axis),
        )
    result = along(cos_table, real_part, 3) - along(sin_table, imag_part, 3)
    return result / float(size**3)


def local_columns(orbitals, points, cinv):
    ranks = lax.axis_size(("grid", "col"))
    local_rows = orbitals.shape[0]
    orbital_count = orbitals.shape[1]
    npoints = cinv.shape[0]
    columns = cinv.shape[1]
    per_rank = columns // ranks
    first_row = lax.axis_index(("grid", "col")) * local_rows
    offset = points - first_row
    inside = (offset >= 0) & (offset < local_rows)
    picked = jnp.take(orbitals, jnp.clip(offset, 0, local_rows - 1), axis=0)
    picked = jnp.where(inside[:, None], picked.astype(jnp.float32), 0.0)
    point_rows = lax.psum(picked, ("grid", "col")).astype(jnp.bfloat16)
    scale = 1.0 / math.sqrt(orbital_count)
    block_rows = math.gcd(local_rows, 1152)

    def pair_block(block):
        product = (
            lax.dot_general(
                block, point_rows, (((1,), (1,)), ((), ())), preferred_element_type=jnp.float32
            )
            * scale
        )
        return (product * product).astype(jnp.bfloat16)

    pairs = lax.map(
        pair_block, orbitals.reshape(local_rows // block_rows, block_rows, orbital_count)
    )
    pairs = pairs.reshape(local_rows, npoints)
    theta_cols = lax.dot_general(
        cinv, pairs, (((0,), (1,)), ((), ())), preferred_element_type=jnp.float32
    )
    fields = lax.all_to_all(theta_cols, ("grid", "col"), split_axis=0, concat_axis=1, tiled=True)
    fields = fields.reshape(per_rank, NX, NX, NX)
    potentials = screened_solve(fields).astype(jnp.bfloat16).reshape(per_rank, NX * NX * NX)
    rows_back = lax.all_to_all(potentials, ("grid", "col"), split_axis=1, concat_axis=0, tiled=True)
    factor = math.sqrt(npoints) / float(NX**3)
    halfway = lax.psum_scatter(
        lax.dot_general(
            pairs, rows_back, (((0,), (1,)), ((), ())), preferred_element_type=jnp.float32
        )
        * factor,
        "grid",
        scatter_dimension=0,
        tiled=True,
    )
    coupling = lax.psum_scatter(halfway, "col", scatter_dimension=0, tiled=True)
    return (rows_back, coupling)


AXES = ("grid", "col")
BF16, F32 = jnp.bfloat16, jnp.float32


def basis(size):
    wave = np.arange(size)[:, None]
    cell = np.arange(size)[None, :]
    angle = 2.0 * np.pi * (wave * cell % size) / size
    rows = np.where(2 * wave <= size, np.cos(angle), np.sin(angle)) * np.sqrt(2.0 / size)
    rows[0] = np.sqrt(1.0 / size)
    if size % 2 == 0:
        rows[size // 2] *= np.sqrt(0.5)
    number = np.minimum(np.arange(size), size - np.arange(size))
    return rows, (number * (2.0 * np.pi / size)) ** 2


def split_tables(table):
    high = np.asarray(table, BF16)
    low = np.asarray(table - high.astype(np.float64), BF16)
    both = np.concatenate([high, low], axis=1)
    return jnp.asarray(both), jnp.asarray(np.concatenate([both, high], axis=1))


def dot(left, right):
    return lax.dot_general(left, right, (((1,), (0,)), ((), ())), preferred_element_type=F32)


def apply_exact(table, values):
    return dot(table, jnp.concatenate([values, values], axis=0))


def apply_split(table, values):
    high = values.astype(BF16)
    low = (values - high.astype(F32)).astype(BF16)
    return dot(table, jnp.concatenate([high, high, low], axis=0))


LANES = 128
UNROLL = 2
BLOCK = 256


def across(ref, index, size):
    rows = pl.ds(index, size, stride=size + 1)
    return jnp.concatenate([ref[half, rows, :] for half in range(ref.shape[0])], axis=1)


def put_across(ref, index, size, value):
    rows = pl.ds(index, size, stride=size + 1)
    for half in range(ref.shape[0]):
        ref[half, rows, :] = value[:, half * LANES : (half + 1) * LANES]


def along_line(ref, line, size):
    rows = pl.ds(line * (size + 1), size)
    return jnp.concatenate([ref[half, rows, :] for half in range(ref.shape[0])], axis=1)


def put_line(ref, line, size, value):
    rows = pl.ds(line * (size + 1), size)
    for half in range(ref.shape[0]):
        ref[half, rows, :] = value[:, half * LANES : (half + 1) * LANES]


def fit_kernel(size, scale, single, orb_ref, pts_ref, cinv_ref, table_ref, *rest):
    if not single:
        rest = rest[1:]
    pair_ref, outs, (field, points, shift, theta) = rest[0], rest[1:-4], rest[-4:]
    plane, step = pl.program_id(0), pl.program_id(1)
    rows = orb_ref.shape[0]
    npoints = pts_ref.shape[0]
    thirds = outs[0].shape[1] if single else len(outs)
    table = table_ref[...]

    @pl.when((plane == 0) & (step == 0))
    def _():
        scaled = pts_ref[...].astype(F32) * scale
        points[...] = scaled.astype(BF16)
        square = scaled * scaled
        norm = jnp.sum(square, axis=1, keepdims=True)
        mean = norm * (jnp.sum(norm) / npoints)
        shift[...] = jnp.sum(mean * cinv_ref[...].astype(F32), axis=0, keepdims=True)

    for start in range(0, npoints, BLOCK):
        part = slice(start, start + BLOCK)
        product = lax.dot_general(
            orb_ref[...], points[part], (((1,), (1,)), ((), ())), preferred_element_type=F32
        )
        pair_ref[:, part] = (product * product).astype(BF16)
    theta[...] = dot(pair_ref[...], cinv_ref[...]) - shift[...]
    for line in range(rows // size):
        value = apply_split(table, theta[line * size : (line + 1) * size])
        put_line(field, step * (rows // size) + line, size, value)

    @pl.when(step == pl.num_programs(1) - 1)
    def _():
        def body(owner, carry):
            for third in range(thirds):
                value = across(field, owner * thirds + third, size)
                value = apply_split(table, value).astype(BF16)
                if single:
                    outs[0][owner, third] = value
                else:
                    outs[third][owner, plane] = value
            return carry

        lax.fori_loop(0, size // thirds, body, 0, unroll=UNROLL)


def solve_kernel(size, passed, wave_b_ref, wave_c_ref, wave_a_ref, table_ref, back_ref, *rest):
    first_ref, rest_ref = rest[:2]
    outs, field = rest[2 + passed : -1], rest[-1]
    owners, later = rest_ref.shape[:2]
    planes = later + 1

    def widen(owner, carry):
        for plane in range(planes):
            value = first_ref[owner, 0] if plane == 0 else rest_ref[owner, plane - 1]
            put_line(field, plane * owners + owner, size, value.astype(F32))
        return carry

    lax.fori_loop(0, owners, widen, 0)
    table, back = table_ref[...], back_ref[...]
    wave_a = wave_a_ref[...]

    def body(mode, carry):
        value = apply_exact(table, across(field, mode, size).astype(BF16))
        squared = wave_a + (wave_b_ref[mode] + wave_c_ref[0])
        weight = jnp.where(squared > 0, 1.0 / (squared + screening), 0.0)
        put_across(field, mode, size, apply_split(back, value * weight))
        return carry

    lax.fori_loop(0, size, body, 0, unroll=UNROLL)

    def narrow(owner, carry):
        for plane in range(planes):
            value = along_line(field, plane * owners + owner, size).astype(BF16)
            if len(outs) == 1:
                outs[0][owner, plane] = value
            elif plane < later:
                outs[0][owner, 0, plane] = value
            else:
                outs[1][owner, 0] = value
        return carry

    lax.fori_loop(0, owners, narrow, 0)


def couple_kernel(size, first, last, factor, *rest):
    first_ref, rest_ref, exact_ref, table_ref, pair_ref = rest[:5]
    rest = rest[5:]
    if not first:
        before_ref, rest = rest[0], rest[2:]
    out_ref, total_ref, field, block, total = rest
    step = pl.program_id(0)
    table = table_ref[...]
    rows = pair_ref.shape[0]
    owners, later = rest_ref.shape[:2]

    @pl.when(step == 0)
    def _():
        if first:
            total[...] = jnp.zeros_like(total)
        else:
            total[...] = before_ref[...]

        def body(owner, carry):
            for third in range(later + 1):
                if third == 0:
                    value = first_ref[owner, 0]
                elif last:
                    value = rest_ref[owner, third - 1]
                else:
                    value = rest_ref[owner, third - 1, 0]
                value = apply_exact(exact_ref[...], value)
                put_across(field, owner * (later + 1) + third, size, value)
            return carry

        lax.fori_loop(0, owners, body, 0, unroll=UNROLL)

    for line in range(rows // size):
        value = along_line(field, step * (rows // size) + line, size)
        block[line * size : (line + 1) * size, :] = apply_split(table, value)
    turned = block[...].T.astype(BF16)
    out_ref[...] = turned
    total[...] += dot(turned, pair_ref[...])

    @pl.when(step == pl.num_programs(0) - 1)
    def _():
        if last:
            total_ref[...] = total[...].T * factor
        else:
            total_ref[...] = total[...]


def const_spec(shape):
    return pl.BlockSpec(shape, lambda *_: (0,) * len(shape))


def cost(flops, moved):
    return pl.CostEstimate(flops=int(flops), bytes_accessed=int(moved), transcendentals=0)


VMEM = 60000 * 1024


def row_blocks(size, lines):
    while size % lines:
        lines -= 1
    return lines * size, size // lines


def local_planes(orbitals, points, cinv):
    size = NX
    ranks = lax.axis_size(AXES)
    rank = lax.axis_index(AXES)
    local_rows, orbital_count = orbitals.shape
    npoints, columns = cinv.shape
    plane_rows = size * size
    planes = local_rows // plane_rows
    later = planes - 1
    halves = columns // LANES

    arrivals = []

    def exchange(array, *after):
        if arrivals:
            array, *_ = lax.optimization_barrier((array, arrivals[-1], *after))
        arrivals.append(lax.all_to_all(array, AXES, 0, 0, tiled=True))
        return arrivals[-1]

    offset = points - rank * local_rows
    inside = (offset >= 0) & (offset < local_rows)
    picked = jnp.take(orbitals, jnp.clip(offset, 0, local_rows - 1), axis=0)
    picked = jnp.where(inside[:, None], picked, jnp.zeros_like(picked))
    shares = exchange(picked.reshape(ranks, npoints // ranks, orbital_count))
    share = jnp.sum(shares.astype(F32), axis=0).astype(BF16)
    point_rows = exchange(jnp.broadcast_to(share[None], shares.shape))
    point_rows = point_rows.reshape(npoints, orbital_count)

    rows, squared = basis(size)
    _, forward = split_tables(rows)
    inverse_exact, inverse = split_tables(rows.T)
    order = (np.arange(ranks)[None, :] * planes + np.arange(planes)[:, None]).reshape(-1)
    forward_a, _ = split_tables(rows[:, order])
    _, inverse_a = split_tables(rows.T[order])
    wave = jnp.asarray(squared, F32)
    wave_a = jnp.asarray(np.broadcast_to(squared[:, None], (size, columns)), F32)

    block_rows, steps = row_blocks(size, 16)
    scale = 1.0 / math.sqrt(orbital_count)
    transform = 2 * 3 * plane_rows * size * columns
    tile = (size, columns)

    smem = pl.BlockSpec(memory_space=pltpu.SMEM)
    anywhere = pl.BlockSpec(memory_space=pl.ANY)

    def fit(start, count, *after):
        shape = (ranks, planes if count == 1 else count, *tile)
        outs = 1 if count == 1 else planes
        pair, *sent = pl.pallas_call(
            functools.partial(fit_kernel, size, scale, count == 1),
            grid=(count, steps),
            in_specs=[
                pl.BlockSpec((block_rows, orbital_count), lambda p, i: ((start + p) * steps + i, 0)),
                const_spec((npoints, orbital_count)),
                const_spec((npoints, columns)),
                const_spec(forward.shape),
            ]
            + [anywhere] * len(after),
            out_specs=[pl.BlockSpec((block_rows, npoints), lambda p, i: (p * steps + i, 0))]
            + [const_spec(shape)] * outs,
            out_shape=[jax.ShapeDtypeStruct((count * plane_rows, npoints), BF16)]
            + [jax.ShapeDtypeStruct(shape, BF16)] * outs,
            scratch_shapes=[
                pltpu.VMEM((halves, size * (size + 1), LANES), F32),
                pltpu.VMEM((npoints, orbital_count), BF16),
                pltpu.VMEM((1, columns), F32),
                pltpu.VMEM((block_rows, columns), F32),
            ],
            compiler_params=pltpu.CompilerParams(
                dimension_semantics=("arbitrary", "arbitrary"), vmem_limit_bytes=VMEM
            ),
            cost_estimate=cost(
                count * (2 * plane_rows * npoints * (orbital_count + columns) + 2 * transform),
                count * plane_rows * (2 * orbital_count + 2 * npoints + 2 * columns),
            ),
            name="fit",
        )(orbitals, point_rows, cinv, forward, *after)
        return pair, sent

    pair_first, (sent_first,) = fit(0, 1)
    arrived_first = exchange(sent_first)
    pair_rest, sent_rest = fit(1, later, pair_first)

    arrived_rest = [exchange(value) for value in sent_rest[:2]]
    back_first = back_rest = arrived_back = None
    for third in range(planes):
        if third > 0 and third + 1 < planes:
            arrived_rest.append(exchange(sent_rest[third + 1], back_first if third == 1 else back_rest[0]))
        arrived = arrived_rest[third]
        wave_c = lax.dynamic_slice(wave, (rank * planes + third,), (1,))
        operands = [wave, wave_c, wave_a, forward_a, inverse_a, arrived_first, arrived]
        in_specs = [smem, smem] + [const_spec(value.shape) for value in operands[2:5]]
        in_specs += [
            pl.BlockSpec((ranks, 1, *tile), lambda i, third=third: (0, third, 0, 0)),
            const_spec((ranks, later, *tile)),
        ]
        passed, aliases = 0, {}
        if third == 0:
            shapes = [(ranks, planes, *tile)]
            out_specs = [const_spec(shapes[0])]
        else:
            shapes = [(ranks, later, later, *tile), (ranks, later, *tile)]
            out_specs = [
                pl.BlockSpec((ranks, 1, later, *tile), lambda i, third=third: (0, third - 1, 0, 0, 0)),
                pl.BlockSpec((ranks, 1, *tile), lambda i, third=third: (0, third - 1, 0, 0)),
            ]
            if third > 1:
                passed = len(back_rest)
                aliases = {len(operands) + k: k for k in range(passed)}
                operands += back_rest
                in_specs += [anywhere] * passed
        result = pl.pallas_call(
            functools.partial(solve_kernel, size, passed),
            grid=(1,),
            in_specs=in_specs,
            out_specs=out_specs,
            out_shape=[jax.ShapeDtypeStruct(shape, BF16) for shape in shapes],
            scratch_shapes=[pltpu.VMEM((halves, size * (size + 1), LANES), F32)],
            input_output_aliases=aliases,
            compiler_params=pltpu.CompilerParams(vmem_limit_bytes=VMEM),
            cost_estimate=cost(2 * transform, 4 * plane_rows * columns),
            name="solve",
        )(*operands)
        if third == 0:
            back_first = result[0]
        else:
            back_rest = result
        if third == max(planes - 2, 0):
            arrived_back = exchange(back_first, result[0])

    back_first = arrived_back
    back_rest = [exchange(value) for value in back_rest]

    factor = math.sqrt(npoints) / float(size**3)
    block_rows, steps = row_blocks(size, 8)
    potential = total = None
    for plane in range(planes):
        first, last = plane == 0, plane == planes - 1
        pair_start = 0 if first else (plane - 1) * steps
        if last:
            rest_spec = const_spec((ranks, later, *tile))
        else:
            rest_spec = pl.BlockSpec(
                (ranks, later, 1, *tile), lambda i, plane=plane: (0, 0, plane, 0, 0)
            )
        in_specs = [
            pl.BlockSpec((ranks, 1, *tile), lambda i, plane=plane: (0, plane, 0, 0)),
            rest_spec,
            const_spec(inverse_exact.shape),
            const_spec(inverse.shape),
            pl.BlockSpec((block_rows, npoints), lambda i, start=pair_start: (start + i, 0)),
        ]
        operands = [back_first, back_rest[last], inverse_exact, inverse, pair_first if first else pair_rest]
        if not first:
            in_specs += [const_spec(total.shape), anywhere]
            operands += [total, potential]
        total_shape = (npoints, columns) if last else (columns, npoints)
        potential, total = pl.pallas_call(
            functools.partial(couple_kernel, size, first, last, factor),
            grid=(steps,),
            in_specs=in_specs,
            out_specs=[
                pl.BlockSpec((columns, block_rows), lambda i, plane=plane: (0, plane * steps + i)),
                const_spec(total_shape),
            ],
            out_shape=[
                jax.ShapeDtypeStruct((columns, local_rows), BF16),
                jax.ShapeDtypeStruct(total_shape, F32),
            ],
            scratch_shapes=[
                pltpu.VMEM((halves, size * (size + 1), LANES), F32),
                pltpu.VMEM((block_rows, columns), F32),
                pltpu.VMEM((columns, npoints), F32),
            ],
            input_output_aliases={} if first else {len(operands) - 1: 0},
            compiler_params=pltpu.CompilerParams(
                dimension_semantics=("arbitrary",), vmem_limit_bytes=VMEM
            ),
            cost_estimate=cost(
                2 * plane_rows * npoints * columns + 2 * transform,
                plane_rows * (2 * npoints + 4 * columns),
            ),
            name="couple",
        )(*operands)

    shares = exchange(total.reshape(ranks, npoints // ranks, columns))
    return potential, jnp.sum(shares, axis=0)


def local(orbitals, points, cinv):
    size = NX
    ranks = lax.axis_size(AXES)
    rows, orbital_count = orbitals.shape
    npoints, columns = cinv.shape
    whole = rows * ranks == size**3 and rows % (size * size) == 0 and size % 16 == 0
    whole = whole and rows >= 2 * size * size
    exact = math.frexp(1.0 / math.sqrt(orbital_count))[0] == 0.5
    if whole and exact and columns % LANES == 0 and npoints % (ranks * 8) == 0:
        return local_planes(orbitals, points, cinv)
    return local_columns(orbitals, points, cinv)


def solution(mesh):
    in_specs = (P(("grid", "col"), None), P(), P())
    out_specs = (P(None, ("grid", "col")), P(("grid", "col"), None))
    return jax.shard_map(local, mesh=mesh, in_specs=in_specs, out_specs=out_specs, check_vma=False)
```

```python
import functools
import math

import jax
import jax.numpy as jnp
import numpy as np
from jax import lax
from jax.experimental import pallas as pl
from jax.experimental.pallas import tpu as pltpu
from jax.sharding import PartitionSpec as P

NX = 96


screening = 0.25


def kernel_table(size):
    index = jnp.arange(size)
    wave = jnp.where(index < (size + 1) // 2, index, index - size).astype(jnp.float32) * (
        2.0 * math.pi / size
    )
    squared = wave[:, None, None] ** 2 + wave[None, :, None] ** 2 + wave[None, None, :] ** 2
    return jnp.where(squared > 0, 1.0 / (squared + screening), 0.0)


def along(table, values, axis):
    forms = {1: "kn,cnyz->ckyz", 2: "kn,cxnz->cxkz", 3: "kn,cxyn->cxyk"}
    return jnp.einsum(forms[axis], table, values, precision=lax.Precision.HIGHEST)


def screened_solve(field):
    size = field.shape[1]
    index = jnp.arange(size, dtype=jnp.int32)
    phase = index[:, None] * index[None, :] % size
    angle = phase.astype(jnp.float32) * (2.0 * math.pi / size)
    cos_table = jnp.cos(angle)
    sin_table = jnp.sin(angle)
    real_part = along(cos_table, field, 3)
    imag_part = -along(sin_table, field, 3)
    for axis in (2, 1):
        real_part, imag_part = (
            along(cos_table, real_part, axis) + along(sin_table, imag_part, axis),
            along(cos_table, imag_part, axis) - along(sin_table, real_part, axis),
        )
    weights = kernel_table(size)
    real_part = real_part * weights
    imag_part = imag_part * weights
    for axis in (1, 2):
        real_part, imag_part = (
            along(cos_table, real_part, axis) - along(sin_table, imag_part, axis),
            along(cos_table, imag_part, axis) + along(sin_table, real_part, axis),
        )
    result = along(cos_table, real_part, 3) - along(sin_table, imag_part, 3)
    return result / float(size**3)


def local_columns(orbitals, points, cinv):
    ranks = lax.axis_size(("grid", "col"))
    local_rows = orbitals.shape[0]
    orbital_count = orbitals.shape[1]
    npoints = cinv.shape[0]
    columns = cinv.shape[1]
    per_rank = columns // ranks
    first_row = lax.axis_index(("grid", "col")) * local_rows
    offset = points - first_row
    inside = (offset >= 0) & (offset < local_rows)
    picked = jnp.take(orbitals, jnp.clip(offset, 0, local_rows - 1), axis=0)
    picked = jnp.where(inside[:, None], picked.astype(jnp.float32), 0.0)
    point_rows = lax.psum(picked, ("grid", "col")).astype(jnp.bfloat16)
    scale = 1.0 / math.sqrt(orbital_count)
    block_rows = math.gcd(local_rows, 1152)

    def pair_block(block):
        product = (
            lax.dot_general(
                block, point_rows, (((1,), (1,)), ((), ())), preferred_element_type=jnp.float32
            )
            * scale
        )
        return (product * product).astype(jnp.bfloat16)

    pairs = lax.map(
        pair_block, orbitals.reshape(local_rows // block_rows, block_rows, orbital_count)
    )
    pairs = pairs.reshape(local_rows, npoints)
    theta_cols = lax.dot_general(
        cinv, pairs, (((0,), (1,)), ((), ())), preferred_element_type=jnp.float32
    )
    fields = lax.all_to_all(theta_cols, ("grid", "col"), split_axis=0, concat_axis=1, tiled=True)
    fields = fields.reshape(per_rank, NX, NX, NX)
    potentials = screened_solve(fields).astype(jnp.bfloat16).reshape(per_rank, NX * NX * NX)
    rows_back = lax.all_to_all(potentials, ("grid", "col"), split_axis=1, concat_axis=0, tiled=True)
    factor = math.sqrt(npoints) / float(NX**3)
    halfway = lax.psum_scatter(
        lax.dot_general(
            pairs, rows_back, (((0,), (1,)), ((), ())), preferred_element_type=jnp.float32
        )
        * factor,
        "grid",
        scatter_dimension=0,
        tiled=True,
    )
    coupling = lax.psum_scatter(halfway, "col", scatter_dimension=0, tiled=True)
    return (rows_back, coupling)


AXES = ("grid", "col")
BF16, F32 = jnp.bfloat16, jnp.float32


def basis(size):
    wave = np.arange(size)[:, None]
    cell = np.arange(size)[None, :]
    angle = 2.0 * np.pi * (wave * cell % size) / size
    rows = np.where(2 * wave <= size, np.cos(angle), np.sin(angle)) * np.sqrt(2.0 / size)
    rows[0] = np.sqrt(1.0 / size)
    if size % 2 == 0:
        rows[size // 2] *= np.sqrt(0.5)
    number = np.minimum(np.arange(size), size - np.arange(size))
    return rows, (number * (2.0 * np.pi / size)) ** 2


def split_tables(table):
    high = np.asarray(table, BF16)
    low = np.asarray(table - high.astype(np.float64), BF16)
    both = np.concatenate([high, low], axis=1)
    return jnp.asarray(both), jnp.asarray(np.concatenate([both, high], axis=1))


def dot(left, right):
    return lax.dot_general(left, right, (((1,), (0,)), ((), ())), preferred_element_type=F32)


def apply_exact(table, values):
    return dot(table, jnp.concatenate([values, values], axis=0))


def apply_split(table, values):
    high = values.astype(BF16)
    low = (values - high.astype(F32)).astype(BF16)
    return dot(table, jnp.concatenate([high, high, low], axis=0))


LANES = 128
UNROLL = 2
BLOCK = 256


def across(ref, index, size):
    rows = pl.ds(index, size, stride=size + 1)
    return jnp.concatenate([ref[half, rows, :] for half in range(ref.shape[0])], axis=1)


def put_across(ref, index, size, value):
    rows = pl.ds(index, size, stride=size + 1)
    for half in range(ref.shape[0]):
        ref[half, rows, :] = value[:, half * LANES : (half + 1) * LANES]


def along_line(ref, line, size):
    rows = pl.ds(line * (size + 1), size)
    return jnp.concatenate([ref[half, rows, :] for half in range(ref.shape[0])], axis=1)


def put_line(ref, line, size, value):
    rows = pl.ds(line * (size + 1), size)
    for half in range(ref.shape[0]):
        ref[half, rows, :] = value[:, half * LANES : (half + 1) * LANES]


def fit_kernel(size, scale, single, orb_ref, pts_ref, cinv_ref, table_ref, *rest):
    if not single:
        rest = rest[1:]
    pair_ref, outs, (field, points, shift, theta) = rest[0], rest[1:-4], rest[-4:]
    plane, step = pl.program_id(0), pl.program_id(1)
    rows = orb_ref.shape[0]
    npoints = pts_ref.shape[0]
    thirds = outs[0].shape[1] + (0 if single else 1)
    table = table_ref[...]

    @pl.when((plane == 0) & (step == 0))
    def _():
        scaled = pts_ref[...].astype(F32) * scale
        points[...] = scaled.astype(BF16)
        square = scaled * scaled
        norm = jnp.sum(square, axis=1, keepdims=True)
        mean = norm * (jnp.sum(norm) / npoints)
        shift[...] = jnp.sum(mean * cinv_ref[...].astype(F32), axis=0, keepdims=True)

    for start in range(0, npoints, BLOCK):
        part = slice(start, start + BLOCK)
        product = lax.dot_general(
            orb_ref[...], points[part], (((1,), (1,)), ((), ())), preferred_element_type=F32
        )
        pair_ref[:, part] = (product * product).astype(BF16)
    theta[...] = dot(pair_ref[...], cinv_ref[...]) - shift[...]
    for line in range(rows // size):
        value = apply_split(table, theta[line * size : (line + 1) * size])
        put_line(field, step * (rows // size) + line, size, value)

    @pl.when(step == pl.num_programs(1) - 1)
    def _():
        def body(owner, carry):
            for third in range(thirds):
                value = across(field, owner * thirds + third, size)
                value = apply_split(table, value).astype(BF16)
                if single:
                    outs[0][owner, third] = value
                elif third < thirds - 1:
                    outs[0][owner, third, plane] = value
                else:
                    outs[1][owner, plane] = value
            return carry

        lax.fori_loop(0, size // thirds, body, 0, unroll=UNROLL)


def solve_kernel(size, start, passed, wave_b_ref, wave_c_ref, wave_a_ref, table_ref, back_ref, *rest):
    first_ref, rest_ref = rest[:2]
    most_ref, last_ref, field = rest[2 + passed :]
    whole = start > 0
    owners, later = rest_ref.shape[0], rest_ref.shape[1 if whole else 2]
    wave_c = wave_c_ref[start + pl.program_id(0)]

    def widen(owner, carry):
        for plane in range(later + 1):
            if plane == 0:
                value = first_ref[owner, 0]
            else:
                value = rest_ref[owner, plane - 1] if whole else rest_ref[owner, 0, plane - 1]
            put_line(field, plane * owners + owner, size, value.astype(F32))
        return carry

    lax.fori_loop(0, owners, widen, 0)
    table, back = table_ref[...], back_ref[...]
    wave_a = wave_a_ref[...]

    def body(mode, carry):
        value = apply_exact(table, across(field, mode, size).astype(BF16))
        squared = wave_a + (wave_b_ref[mode] + wave_c)
        weight = jnp.where(squared > 0, 1.0 / (squared + screening), 0.0)
        put_across(field, mode, size, apply_split(back, value * weight))
        return carry

    lax.fori_loop(0, size, body, 0, unroll=UNROLL)

    def narrow(owner, carry):
        for plane in range(later + 1):
            value = along_line(field, plane * owners + owner, size).astype(BF16)
            if plane == later:
                last_ref[owner, 0] = value
            elif whole:
                most_ref[owner, plane] = value
            else:
                most_ref[owner, 0, plane] = value
        return carry

    lax.fori_loop(0, owners, narrow, 0)


def couple_kernel(size, first, last, factor, *rest):
    count = 1 if last else 2
    sources, (exact_ref, table_ref, pair_ref) = rest[:count], rest[count : count + 3]
    rest = rest[count + 3 :]
    if not first:
        before_ref, rest = rest[0], rest[2:]
    out_ref, total_ref, field, block, total = rest
    step = pl.program_id(0)
    table = table_ref[...]
    rows = pair_ref.shape[0]
    owners = sources[0].shape[0]
    thirds = size // owners

    @pl.when(step == 0)
    def _():
        if first:
            total[...] = jnp.zeros_like(total)
        else:
            total[...] = before_ref[...]

        def body(owner, carry):
            for third in range(thirds):
                if last:
                    value = sources[0][owner, third]
                elif third < thirds - 1:
                    value = sources[0][owner, third, 0]
                else:
                    value = sources[1][owner, 0]
                value = apply_exact(exact_ref[...], value)
                put_across(field, owner * thirds + third, size, value)
            return carry

        lax.fori_loop(0, owners, body, 0, unroll=UNROLL)

    for line in range(rows // size):
        value = along_line(field, step * (rows // size) + line, size)
        block[line * size : (line + 1) * size, :] = apply_split(table, value)
    turned = block[...].T.astype(BF16)
    out_ref[...] = turned
    total[...] += dot(turned, pair_ref[...])

    @pl.when(step == pl.num_programs(0) - 1)
    def _():
        if last:
            total_ref[...] = total[...].T * factor
        else:
            total_ref[...] = total[...]


def const_spec(shape):
    return pl.BlockSpec(shape, lambda *_: (0,) * len(shape))


def cost(flops, moved):
    return pl.CostEstimate(flops=int(flops), bytes_accessed=int(moved), transcendentals=0)


VMEM = 60000 * 1024


def row_blocks(size, lines):
    while size % lines:
        lines -= 1
    return lines * size, size // lines


def local_planes(orbitals, points, cinv):
    size = NX
    ranks = lax.axis_size(AXES)
    rank = lax.axis_index(AXES)
    local_rows, orbital_count = orbitals.shape
    npoints, columns = cinv.shape
    plane_rows = size * size
    planes = local_rows // plane_rows
    later = planes - 1
    halves = columns // LANES

    arrivals = []

    def exchange(array):
        if arrivals:
            array, _ = lax.optimization_barrier((array, arrivals[-1]))
        arrivals.append(lax.all_to_all(array, AXES, 0, 0, tiled=True))
        return arrivals[-1]

    chips = lax.axis_size("grid")
    core = lax.axis_index("col")

    def swap(array):
        return lax.ppermute(array, "col", [(0, 1), (1, 0)])

    def scatter_sum(array):
        array = array.reshape(chips, 2, npoints // ranks, -1)
        own = lax.dynamic_index_in_dim(array, core, 1, keepdims=False)
        array = own + swap(lax.dynamic_index_in_dim(array, 1 - core, 1, keepdims=False))
        array = lax.all_to_all(array, "grid", 0, 0, tiled=True)
        return jnp.sum(array.astype(F32), axis=0).astype(array.dtype)

    offset = points - rank * local_rows
    inside = (offset >= 0) & (offset < local_rows)
    picked = jnp.take(orbitals, jnp.clip(offset, 0, local_rows - 1), axis=0)
    picked = jnp.where(inside[:, None], picked, jnp.zeros_like(picked))
    share = scatter_sum(picked)
    share = jnp.broadcast_to(share[None], (chips, *share.shape))
    own = lax.all_to_all(share, "grid", 0, 0, tiled=True)
    both = jnp.stack([own, swap(own)], axis=1)
    point_rows = jnp.where(core == 0, both, both[:, ::-1]).reshape(npoints, orbital_count)

    rows, squared = basis(size)
    _, forward = split_tables(rows)
    inverse_exact, inverse = split_tables(rows.T)
    order = (np.arange(ranks)[None, :] * planes + np.arange(planes)[:, None]).reshape(-1)
    forward_a, _ = split_tables(rows[:, order])
    _, inverse_a = split_tables(rows.T[order])
    wave = jnp.asarray(squared, F32)
    wave_a = jnp.asarray(np.broadcast_to(squared[:, None], (size, columns)), F32)

    block_rows, steps = row_blocks(size, 16)
    scale = 1.0 / math.sqrt(orbital_count)
    transform = 2 * 3 * plane_rows * size * columns
    tile = (size, columns)

    smem = pl.BlockSpec(memory_space=pltpu.SMEM)
    anywhere = pl.BlockSpec(memory_space=pl.ANY)

    def fit(start, count, *after):
        if count == 1 and start == 0:
            shapes = [(ranks, planes, *tile)]
        else:
            shapes = [(ranks, planes - 1, count, *tile), (ranks, count, *tile)]
        pair, *sent = pl.pallas_call(
            functools.partial(fit_kernel, size, scale, start == 0),
            grid=(count, steps),
            in_specs=[
                pl.BlockSpec((block_rows, orbital_count), lambda p, i: ((start + p) * steps + i, 0)),
                const_spec((npoints, orbital_count)),
                const_spec((npoints, columns)),
                const_spec(forward.shape),
            ]
            + [anywhere] * len(after),
            out_specs=[pl.BlockSpec((block_rows, npoints), lambda p, i: (p * steps + i, 0))]
            + [const_spec(shape) for shape in shapes],
            out_shape=[jax.ShapeDtypeStruct((count * plane_rows, npoints), BF16)]
            + [jax.ShapeDtypeStruct(shape, BF16) for shape in shapes],
            scratch_shapes=[
                pltpu.VMEM((halves, size * (size + 1), LANES), F32),
                pltpu.VMEM((npoints, orbital_count), BF16),
                pltpu.VMEM((1, columns), F32),
                pltpu.VMEM((block_rows, columns), F32),
            ],
            compiler_params=pltpu.CompilerParams(
                dimension_semantics=("arbitrary", "arbitrary"), vmem_limit_bytes=VMEM
            ),
            cost_estimate=cost(
                count * (2 * plane_rows * npoints * (orbital_count + columns) + 2 * transform),
                count * plane_rows * (2 * orbital_count + 2 * npoints + 2 * columns),
            ),
            name="fit",
        )(orbitals, point_rows, cinv, forward, *after)
        return pair, sent

    pair_first, (sent_first,) = fit(0, 1)
    arrived_first = exchange(sent_first)
    pair_rest, sent_rest = fit(1, later, pair_first)
    arrived_most, arrived_last = [exchange(value) for value in sent_rest]

    wave_c = lax.dynamic_slice(wave, (rank * planes,), (planes,))

    def solve(start, count, arrived, *passed):
        operands = [wave, wave_c, wave_a, forward_a, inverse_a, arrived_first, arrived, *passed]
        third_spec = pl.BlockSpec((ranks, 1, *tile), lambda i: (0, start + i, 0, 0))
        if start > 0:
            most_shape = (ranks, later, *tile)
            most_spec = const_spec(most_shape)
        else:
            most_shape = (ranks, count, later, *tile)
            most_spec = pl.BlockSpec((ranks, 1, later, *tile), lambda i: (0, i, 0, 0, 0))
        return pl.pallas_call(
            functools.partial(solve_kernel, size, start, len(passed)),
            grid=(count,),
            in_specs=[smem, smem]
            + [const_spec(value.shape) for value in operands[2:5]]
            + [third_spec, most_spec]
            + [anywhere] * len(passed),
            out_specs=[most_spec, third_spec],
            out_shape=[
                jax.ShapeDtypeStruct(most_shape, BF16),
                jax.ShapeDtypeStruct((ranks, planes, *tile), BF16),
            ],
            scratch_shapes=[pltpu.VMEM((halves, size * (size + 1), LANES), F32)],
            input_output_aliases={7: 1} if passed else {},
            compiler_params=pltpu.CompilerParams(
                dimension_semantics=("arbitrary",), vmem_limit_bytes=VMEM
            ),
            cost_estimate=cost(2 * count * transform, 4 * count * plane_rows * columns),
            name="solve",
        )(*operands)

    back_most, back_end = solve(0, later, arrived_most)
    arrived_most = exchange(back_most)
    back_last, back_end = solve(later, 1, arrived_last, back_end)
    arrived_last = exchange(back_last)
    arrived_end = exchange(back_end)

    factor = math.sqrt(npoints) / float(size**3)
    block_rows, steps = row_blocks(size, 8)
    potential = total = None
    for plane in range(planes):
        first, last = plane == 0, plane == planes - 1
        pair_start = 0 if first else (plane - 1) * steps
        if last:
            sources, in_specs = [arrived_end], [const_spec(arrived_end.shape)]
        else:
            sources = [arrived_most, arrived_last]
            in_specs = [
                pl.BlockSpec((ranks, later, 1, *tile), lambda i, plane=plane: (0, 0, plane, 0, 0)),
                pl.BlockSpec((ranks, 1, *tile), lambda i, plane=plane: (0, plane, 0, 0)),
            ]
        in_specs += [
            const_spec(inverse_exact.shape),
            const_spec(inverse.shape),
            pl.BlockSpec((block_rows, npoints), lambda i, start=pair_start: (start + i, 0)),
        ]
        operands = [*sources, inverse_exact, inverse, pair_first if first else pair_rest]
        if not first:
            in_specs += [const_spec(total.shape), anywhere]
            operands += [total, potential]
        total_shape = (npoints, columns) if last else (columns, npoints)
        potential, total = pl.pallas_call(
            functools.partial(couple_kernel, size, first, last, factor),
            grid=(steps,),
            in_specs=in_specs,
            out_specs=[
                pl.BlockSpec((columns, block_rows), lambda i, plane=plane: (0, plane * steps + i)),
                const_spec(total_shape),
            ],
            out_shape=[
                jax.ShapeDtypeStruct((columns, local_rows), BF16),
                jax.ShapeDtypeStruct(total_shape, F32),
            ],
            scratch_shapes=[
                pltpu.VMEM((halves, size * (size + 1), LANES), F32),
                pltpu.VMEM((block_rows, columns), F32),
                pltpu.VMEM((columns, npoints), F32),
            ],
            input_output_aliases={} if first else {len(operands) - 1: 0},
            compiler_params=pltpu.CompilerParams(
                dimension_semantics=("arbitrary",), vmem_limit_bytes=VMEM
            ),
            cost_estimate=cost(
                2 * plane_rows * npoints * columns + 2 * transform,
                plane_rows * (2 * npoints + 4 * columns),
            ),
            name="couple",
        )(*operands)

    return potential, scatter_sum(total)


def local(orbitals, points, cinv):
    size = NX
    ranks = lax.axis_size(AXES)
    rows, orbital_count = orbitals.shape
    npoints, columns = cinv.shape
    whole = rows * ranks == size**3 and rows % (size * size) == 0 and size % 16 == 0
    whole = whole and rows >= 2 * size * size and lax.axis_size("col") == 2
    exact = math.frexp(1.0 / math.sqrt(orbital_count))[0] == 0.5
    if whole and exact and columns % LANES == 0 and npoints % (ranks * 8) == 0:
        return local_planes(orbitals, points, cinv)
    return local_columns(orbitals, points, cinv)


def solution(mesh):
    in_specs = (P(("grid", "col"), None), P(), P())
    out_specs = (P(None, ("grid", "col")), P(("grid", "col"), None))
    return jax.shard_map(local, mesh=mesh, in_specs=in_specs, out_specs=out_specs, check_vma=False)
```

```python
import functools
import math

import jax
import jax.numpy as jnp
import numpy as np
from jax import lax
from jax.experimental import pallas as pl
from jax.experimental.pallas import tpu as pltpu
from jax.sharding import PartitionSpec as P


NX = 96


screening = 0.25


def kernel_table(size):
    index = jnp.arange(size)
    wave = jnp.where(index < (size + 1) // 2, index, index - size).astype(jnp.float32) * (
        2.0 * math.pi / size
    )
    squared = wave[:, None, None] ** 2 + wave[None, :, None] ** 2 + wave[None, None, :] ** 2
    return jnp.where(squared > 0, 1.0 / (squared + screening), 0.0)


def along(table, values, axis):
    forms = {1: "kn,cnyz->ckyz", 2: "kn,cxnz->cxkz", 3: "kn,cxyn->cxyk"}
    return jnp.einsum(forms[axis], table, values, precision=lax.Precision.HIGHEST)


def screened_solve(field):
    size = field.shape[1]
    index = jnp.arange(size, dtype=jnp.int32)
    phase = index[:, None] * index[None, :] % size
    angle = phase.astype(jnp.float32) * (2.0 * math.pi / size)
    cos_table = jnp.cos(angle)
    sin_table = jnp.sin(angle)
    real_part = along(cos_table, field, 3)
    imag_part = -along(sin_table, field, 3)
    for axis in (2, 1):
        real_part, imag_part = (
            along(cos_table, real_part, axis) + along(sin_table, imag_part, axis),
            along(cos_table, imag_part, axis) - along(sin_table, real_part, axis),
        )
    weights = kernel_table(size)
    real_part = real_part * weights
    imag_part = imag_part * weights
    for axis in (1, 2):
        real_part, imag_part = (
            along(cos_table, real_part, axis) - along(sin_table, imag_part, axis),
            along(cos_table, imag_part, axis) + along(sin_table, real_part, axis),
        )
    result = along(cos_table, real_part, 3) - along(sin_table, imag_part, 3)
    return result / float(size**3)


def local_columns(orbitals, points, cinv):
    ranks = lax.axis_size(("grid", "col"))
    local_rows = orbitals.shape[0]
    orbital_count = orbitals.shape[1]
    npoints = cinv.shape[0]
    columns = cinv.shape[1]
    per_rank = columns // ranks
    first_row = lax.axis_index(("grid", "col")) * local_rows
    offset = points - first_row
    inside = (offset >= 0) & (offset < local_rows)
    picked = jnp.take(orbitals, jnp.clip(offset, 0, local_rows - 1), axis=0)
    picked = jnp.where(inside[:, None], picked.astype(jnp.float32), 0.0)
    point_rows = lax.psum(picked, ("grid", "col")).astype(jnp.bfloat16)
    scale = 1.0 / math.sqrt(orbital_count)
    block_rows = math.gcd(local_rows, 1152)

    def pair_block(block):
        product = (
            lax.dot_general(
                block, point_rows, (((1,), (1,)), ((), ())), preferred_element_type=jnp.float32
            )
            * scale
        )
        return (product * product).astype(jnp.bfloat16)

    pairs = lax.map(
        pair_block, orbitals.reshape(local_rows // block_rows, block_rows, orbital_count)
    )
    pairs = pairs.reshape(local_rows, npoints)
    theta_cols = lax.dot_general(
        cinv, pairs, (((0,), (1,)), ((), ())), preferred_element_type=jnp.float32
    )
    fields = lax.all_to_all(theta_cols, ("grid", "col"), split_axis=0, concat_axis=1, tiled=True)
    fields = fields.reshape(per_rank, NX, NX, NX)
    potentials = screened_solve(fields).astype(jnp.bfloat16).reshape(per_rank, NX * NX * NX)
    rows_back = lax.all_to_all(potentials, ("grid", "col"), split_axis=1, concat_axis=0, tiled=True)
    factor = math.sqrt(npoints) / float(NX**3)
    halfway = lax.psum_scatter(
        lax.dot_general(
            pairs, rows_back, (((0,), (1,)), ((), ())), preferred_element_type=jnp.float32
        )
        * factor,
        "grid",
        scatter_dimension=0,
        tiled=True,
    )
    coupling = lax.psum_scatter(halfway, "col", scatter_dimension=0, tiled=True)
    return (rows_back, coupling)


AXES = ("grid", "col")
BF16, F32 = jnp.bfloat16, jnp.float32


def basis(size):
    wave = np.arange(size)[:, None]
    cell = np.arange(size)[None, :]
    angle = 2.0 * np.pi * (wave * cell % size) / size
    rows = np.where(2 * wave <= size, np.cos(angle), np.sin(angle)) * np.sqrt(2.0 / size)
    rows[0] = np.sqrt(1.0 / size)
    if size % 2 == 0:
        rows[size // 2] *= np.sqrt(0.5)
    number = np.minimum(np.arange(size), size - np.arange(size))
    return rows, (number * (2.0 * np.pi / size)) ** 2


def split_tables(table):
    high = np.asarray(table, BF16)
    low = np.asarray(table - high.astype(np.float64), BF16)
    both = np.concatenate([high, low], axis=1)
    return jnp.asarray(both), jnp.asarray(np.concatenate([both, high], axis=1))


def dot(left, right):
    return lax.dot_general(left, right, (((1,), (0,)), ((), ())), preferred_element_type=F32)


def apply_exact(table, values):
    return dot(table, jnp.concatenate([values, values], axis=0))


def apply_split(table, values):
    high = values.astype(BF16)
    low = (values - high.astype(F32)).astype(BF16)
    return dot(table, jnp.concatenate([high, high, low], axis=0))


LANES = 128
UNROLL = 2
BLOCK = 256


def across(ref, index, size):
    rows = pl.ds(index, size, stride=size + 1)
    return jnp.concatenate([ref[half, rows, :] for half in range(ref.shape[0])], axis=1)


def put_across(ref, index, size, value):
    rows = pl.ds(index, size, stride=size + 1)
    for half in range(ref.shape[0]):
        ref[half, rows, :] = value[:, half * LANES : (half + 1) * LANES]


def along_line(ref, line, size):
    rows = pl.ds(line * (size + 1), size)
    return jnp.concatenate([ref[half, rows, :] for half in range(ref.shape[0])], axis=1)


def put_line(ref, line, size, value):
    rows = pl.ds(line * (size + 1), size)
    for half in range(ref.shape[0]):
        ref[half, rows, :] = value[:, half * LANES : (half + 1) * LANES]


def fit_kernel(size, scale, single, orb_ref, pts_ref, cinv_ref, table_ref, *rest):
    if not single:
        rest = rest[1:]
    pair_ref, outs, (field, points, shift, theta) = rest[0], rest[1:-4], rest[-4:]
    plane, step = pl.program_id(0), pl.program_id(1)
    rows = orb_ref.shape[0]
    npoints = pts_ref.shape[0]
    thirds = outs[0].shape[1] + (0 if single else 1)
    table = table_ref[...]

    @pl.when((plane == 0) & (step == 0))
    def _():
        scaled = pts_ref[...].astype(F32) * scale
        points[...] = scaled.astype(BF16)
        square = scaled * scaled
        norm = jnp.sum(square, axis=1, keepdims=True)
        mean = norm * (jnp.sum(norm) / npoints)
        shift[...] = jnp.sum(mean * cinv_ref[...].astype(F32), axis=0, keepdims=True)

    for start in range(0, npoints, BLOCK):
        part = slice(start, start + BLOCK)
        product = lax.dot_general(
            orb_ref[...], points[part], (((1,), (1,)), ((), ())), preferred_element_type=F32
        )
        pair_ref[:, part] = (product * product).astype(BF16)
    theta[...] = dot(pair_ref[...], cinv_ref[...]) - shift[...]
    for line in range(rows // size):
        value = apply_split(table, theta[line * size : (line + 1) * size])
        put_line(field, step * (rows // size) + line, size, value)

    @pl.when(step == pl.num_programs(1) - 1)
    def _():
        def body(owner, carry):
            for third in range(thirds):
                value = across(field, owner * thirds + third, size)
                value = apply_split(table, value).astype(BF16)
                if single:
                    outs[0][owner, third] = value
                elif third < thirds - 1:
                    outs[0][owner, third, plane] = value
                else:
                    outs[1][owner, plane] = value
            return carry

        lax.fori_loop(0, size // thirds, body, 0, unroll=UNROLL)


def solve_kernel(size, start, passed, wave_b_ref, wave_c_ref, wave_a_ref, table_ref, back_ref, *rest):
    first_ref, rest_ref = rest[:2]
    most_ref, *end_refs, field = rest[2 + passed :]
    whole = start > 0
    owners, later = rest_ref.shape[0], rest_ref.shape[1 if whole else 2]
    wave_c = wave_c_ref[start + pl.program_id(0)]

    def widen(owner, carry):
        for plane in range(later + 1):
            if plane == 0:
                value = first_ref[owner, 0]
            else:
                value = rest_ref[owner, plane - 1] if whole else rest_ref[owner, 0, plane - 1]
            put_line(field, plane * owners + owner, size, value.astype(F32))
        return carry

    lax.fori_loop(0, owners, widen, 0)
    table, back = table_ref[...], back_ref[...]
    wave_a = wave_a_ref[...]

    def body(mode, carry):
        value = apply_exact(table, across(field, mode, size).astype(BF16))
        squared = wave_a + (wave_b_ref[mode] + wave_c)
        weight = jnp.where(squared > 0, 1.0 / (squared + screening), 0.0)
        put_across(field, mode, size, apply_split(back, value * weight))
        return carry

    lax.fori_loop(0, size, body, 0, unroll=UNROLL)

    def narrow(owner, carry):
        for plane in range(later + 1):
            value = along_line(field, plane * owners + owner, size).astype(BF16)
            parts = [value[:, k * LANES : (k + 1) * LANES] for k in range(len(end_refs))]
            if plane == later:
                for end_ref, part in zip(end_refs, parts):
                    end_ref[owner, 0] = part
            elif whole:
                for k, part in enumerate(parts):
                    most_ref[owner, plane * len(parts) + k] = part
            else:
                most_ref[owner, 0, plane] = value
        return carry

    lax.fori_loop(0, owners, narrow, 0)


def couple_kernel(size, count, first, last, factor, *rest):
    sources, (exact_ref, table_ref, pair_ref) = rest[:count], rest[count : count + 3]
    rest = rest[count + 3 :]
    if not first:
        before_ref, rest = rest[0], rest[2:]
    out_ref, total_ref, field, block, total = rest
    step = pl.program_id(0)
    table = table_ref[...]
    rows = pair_ref.shape[0]
    owners = sources[0].shape[0]
    thirds = size // owners

    @pl.when(step == 0)
    def _():
        if first:
            total[...] = jnp.zeros_like(total)
        else:
            total[...] = before_ref[...]

        def body(owner, carry):
            for third in range(thirds):
                if last:
                    value = sources[third][owner, 0]
                elif third < thirds - 1:
                    value = sources[0][owner, third, 0]
                else:
                    parts = [source[owner, 0] for source in sources[1:]]
                    value = jnp.concatenate(parts, axis=1)
                value = apply_exact(exact_ref[...], value)
                put_across(field, owner * thirds + third, size, value)
            return carry

        lax.fori_loop(0, owners, body, 0, unroll=UNROLL)

    for line in range(rows // size):
        value = along_line(field, step * (rows // size) + line, size)
        block[line * size : (line + 1) * size, :] = apply_split(table, value)
    turned = block[...].T.astype(BF16)
    out_ref[...] = turned
    total[...] += dot(turned, pair_ref[...])

    @pl.when(step == pl.num_programs(0) - 1)
    def _():
        if last:
            total_ref[...] = total[...].T * factor
        else:
            total_ref[...] = total[...]


def const_spec(shape):
    return pl.BlockSpec(shape, lambda *_: (0,) * len(shape))


def cost(flops, moved):
    return pl.CostEstimate(flops=int(flops), bytes_accessed=int(moved), transcendentals=0)


VMEM = 65472 * 1024


def row_blocks(size, lines):
    while size % lines:
        lines -= 1
    return lines * size, size // lines


def local_planes(orbitals, points, cinv):
    size = NX
    ranks = lax.axis_size(AXES)
    rank = lax.axis_index(AXES)
    local_rows, orbital_count = orbitals.shape
    npoints, columns = cinv.shape
    plane_rows = size * size
    planes = local_rows // plane_rows
    later = planes - 1
    halves = columns // LANES

    arrivals = []

    def exchange(array):
        if arrivals:
            array, _ = lax.optimization_barrier((array, arrivals[-1]))
        arrivals.append(lax.all_to_all(array, AXES, 0, 0, tiled=True))
        return arrivals[-1]

    chips = lax.axis_size("grid")
    core = lax.axis_index("col")

    def swap(array):
        return lax.ppermute(array, "col", [(0, 1), (1, 0)])

    def pair_sum(array):
        array = array.reshape(chips, 2, npoints // ranks, -1)
        own = lax.dynamic_index_in_dim(array, core, 1, keepdims=False)
        return own + swap(lax.dynamic_index_in_dim(array, 1 - core, 1, keepdims=False))

    def chip_sum(array):
        array = lax.all_to_all(array, "grid", 0, 0, tiled=True)
        return jnp.sum(array.astype(F32), axis=0).astype(array.dtype)

    offset = points - rank * local_rows
    inside = (offset >= 0) & (offset < local_rows)
    picked = jnp.take(orbitals, jnp.clip(offset, 0, local_rows - 1), axis=0)
    picked = jnp.where(inside[:, None], picked, jnp.zeros_like(picked))
    share = chip_sum(pair_sum(picked))
    share = jnp.broadcast_to(share[None], (chips, *share.shape))
    own = lax.all_to_all(share, "grid", 0, 0, tiled=True)
    both = jnp.stack([own, swap(own)], axis=1)
    point_rows = jnp.where(core == 0, both, both[:, ::-1]).reshape(npoints, orbital_count)

    rows, squared = basis(size)
    _, forward = split_tables(rows)
    inverse_exact, inverse = split_tables(rows.T)
    order = (np.arange(ranks)[None, :] * planes + np.arange(planes)[:, None]).reshape(-1)
    forward_a, _ = split_tables(rows[:, order])
    _, inverse_a = split_tables(rows.T[order])
    wave = jnp.asarray(squared, F32)
    wave_a = jnp.asarray(np.broadcast_to(squared[:, None], (size, columns)), F32)

    block_rows, steps = row_blocks(size, 16)
    scale = 1.0 / math.sqrt(orbital_count)
    transform = 2 * 3 * plane_rows * size * columns
    tile, unit = (size, columns), (size, LANES)

    smem = pl.BlockSpec(memory_space=pltpu.SMEM)
    anywhere = pl.BlockSpec(memory_space=pl.ANY)

    def fit(start, count, *after):
        if count == 1 and start == 0:
            shapes = [(ranks, planes, *tile)]
        else:
            shapes = [(ranks, planes - 1, count, *tile), (ranks, count, *tile)]
        pair, *sent = pl.pallas_call(
            functools.partial(fit_kernel, size, scale, start == 0),
            grid=(count, steps),
            in_specs=[
                pl.BlockSpec((block_rows, orbital_count), lambda p, i: ((start + p) * steps + i, 0)),
                const_spec((npoints, orbital_count)),
                const_spec((npoints, columns)),
                const_spec(forward.shape),
            ]
            + [anywhere] * len(after),
            out_specs=[pl.BlockSpec((block_rows, npoints), lambda p, i: (p * steps + i, 0))]
            + [const_spec(shape) for shape in shapes],
            out_shape=[jax.ShapeDtypeStruct((count * plane_rows, npoints), BF16)]
            + [jax.ShapeDtypeStruct(shape, BF16) for shape in shapes],
            scratch_shapes=[
                pltpu.VMEM((halves, size * (size + 1), LANES), F32),
                pltpu.VMEM((npoints, orbital_count), BF16),
                pltpu.VMEM((1, columns), F32),
                pltpu.VMEM((block_rows, columns), F32),
            ],
            compiler_params=pltpu.CompilerParams(
                dimension_semantics=("arbitrary", "arbitrary"), vmem_limit_bytes=VMEM
            ),
            cost_estimate=cost(
                count * (2 * plane_rows * npoints * (orbital_count + columns) + 2 * transform),
                count * plane_rows * (2 * orbital_count + 2 * npoints + 2 * columns),
            ),
            name="fit",
        )(orbitals, point_rows, cinv, forward, *after)
        return pair, sent

    pair_first, (sent_first,) = fit(0, 1)
    arrived_first = exchange(sent_first)
    pair_rest, sent_rest = fit(1, later, pair_first)
    arrived_most, arrived_last = [exchange(value) for value in sent_rest]

    wave_c = lax.dynamic_slice(wave, (rank * planes,), (planes,))

    def solve(start, count, arrived, *passed):
        operands = [wave, wave_c, wave_a, forward_a, inverse_a, arrived_first, arrived, *passed]
        third_spec = pl.BlockSpec((ranks, 1, *tile), lambda i: (0, start + i, 0, 0))
        end_spec = pl.BlockSpec((ranks, 1, *unit), lambda i: (0, start + i, 0, 0))
        if start > 0:
            most_shape = (ranks, later * halves, *unit)
            most_spec = const_spec(most_shape)
            rest_spec = const_spec(arrived.shape)
        else:
            most_shape = (ranks, count, later, *tile)
            most_spec = rest_spec = pl.BlockSpec(
                (ranks, 1, later, *tile), lambda i: (0, i, 0, 0, 0)
            )
        return pl.pallas_call(
            functools.partial(solve_kernel, size, start, len(passed)),
            grid=(count,),
            in_specs=[smem, smem]
            + [const_spec(value.shape) for value in operands[2:5]]
            + [third_spec, rest_spec]
            + [anywhere] * len(passed),
            out_specs=[most_spec] + [end_spec] * halves,
            out_shape=[jax.ShapeDtypeStruct(most_shape, BF16)]
            + [jax.ShapeDtypeStruct((ranks, planes, *unit), BF16)] * halves,
            scratch_shapes=[pltpu.VMEM((halves, size * (size + 1), LANES), F32)],
            input_output_aliases={7 + k: 1 + k for k in range(len(passed))},
            compiler_params=pltpu.CompilerParams(
                dimension_semantics=("arbitrary",), vmem_limit_bytes=VMEM
            ),
            cost_estimate=cost(2 * count * transform, 4 * count * plane_rows * columns),
            name="solve",
        )(*operands)

    back_most, *back_ends = solve(0, later, arrived_most)
    arrived_most = exchange(back_most)
    back_last, *back_ends = solve(later, 1, arrived_last, *back_ends)
    arrived_last = exchange(jnp.concatenate([back_last, *back_ends[:-1]], axis=1))
    arrived_end = exchange(back_ends[-1])

    factor = math.sqrt(npoints) / float(size**3)
    block_rows, steps = row_blocks(size, 8)
    calls = [(plane, 0, columns) for plane in range(later)]
    calls += [(later, half, LANES) for half in range(halves)]
    potential = total = None
    ends = []
    for plane, part, width in calls:
        first, last = plane == 0, plane == later

        def unit_spec(index):
            return pl.BlockSpec((ranks, 1, *unit), lambda i: (0, index, 0, 0))

        if not last:
            sources = [arrived_most] + [arrived_last] * halves
            in_specs = [
                pl.BlockSpec((ranks, later, 1, *tile), lambda i, plane=plane: (0, 0, plane, 0, 0))
            ]
            in_specs += [unit_spec(plane * halves + k) for k in range(halves)]
        elif part < halves - 1:
            sources = [arrived_last] * planes
            in_specs = [unit_spec(later * halves + part * planes + k) for k in range(planes)]
        else:
            if ends:
                arrived_end, _ = lax.optimization_barrier((arrived_end, ends[-1]))
            sources = [arrived_end] * planes
            in_specs = [unit_spec(k) for k in range(planes)]
        pair_start = 0 if first else (plane - 1) * steps
        in_specs += [
            const_spec(inverse_exact.shape),
            const_spec(inverse.shape),
            pl.BlockSpec((block_rows, npoints), lambda i, start=pair_start: (start + i, 0)),
        ]
        operands = [*sources, inverse_exact, inverse, pair_first if first else pair_rest]
        if not first:
            in_specs += [pl.BlockSpec((width, npoints), lambda i, part=part: (part, 0)), anywhere]
            operands += [total, potential]
        total_shape = (npoints, width) if last else (columns, npoints)
        call = pl.pallas_call(
            functools.partial(couple_kernel, size, len(sources), first, last, factor),
            grid=(steps,),
            in_specs=in_specs,
            out_specs=[
                pl.BlockSpec(
                    (width, block_rows),
                    lambda i, plane=plane, part=part: (part, plane * steps + i),
                ),
                const_spec(total_shape),
            ],
            out_shape=[
                jax.ShapeDtypeStruct((columns, local_rows), BF16),
                jax.ShapeDtypeStruct(total_shape, F32),
            ],
            scratch_shapes=[
                pltpu.VMEM((width // LANES, size * (size + 1), LANES), F32),
                pltpu.VMEM((block_rows, width), F32),
                pltpu.VMEM((width, npoints), F32),
            ],
            input_output_aliases={} if first else {len(operands) - 1: 0},
            compiler_params=pltpu.CompilerParams(
                dimension_semantics=("arbitrary",), vmem_limit_bytes=VMEM
            ),
            cost_estimate=cost(
                2 * plane_rows * npoints * width + 2 * transform * width // columns,
                plane_rows * (2 * npoints + 4 * width),
            ),
            name="couple",
        )
        potential, result = call(*operands)
        if last:
            ends.append(pair_sum(result))
        else:
            total = result
    for half, end in enumerate(ends):
        shares = lax.all_to_all(end, "grid", 0, 0, tiled=True)
        ends[half] = jnp.sum(shares, axis=0)
    return potential, jnp.concatenate(ends, axis=1)


def local(orbitals, points, cinv):
    size = NX
    ranks = lax.axis_size(AXES)
    rows, orbital_count = orbitals.shape
    npoints, columns = cinv.shape
    whole = rows * ranks == size**3 and rows % (size * size) == 0 and size % 16 == 0
    whole = whole and rows >= 2 * size * size and lax.axis_size("col") == 2
    exact = math.frexp(1.0 / math.sqrt(orbital_count))[0] == 0.5
    if whole and exact and columns % LANES == 0 and npoints % (ranks * 8) == 0:
        return local_planes(orbitals, points, cinv)
    return local_columns(orbitals, points, cinv)


def solution(mesh):
    in_specs = (P(("grid", "col"), None), P(), P())
    out_specs = (P(None, ("grid", "col")), P(("grid", "col"), None))
    return jax.shard_map(
        local, mesh=mesh, in_specs=in_specs, out_specs=out_specs, check_vma=False
    )
```

```python
import functools
import math

import jax
import jax.numpy as jnp
import numpy as np
from jax import lax
from jax.experimental import pallas as pl
from jax.experimental.pallas import tpu as pltpu
from jax.sharding import PartitionSpec as P

NX = 96


screening = 0.25


def kernel_table(size):
    index = jnp.arange(size)
    wave = jnp.where(index < (size + 1) // 2, index, index - size).astype(jnp.float32) * (
        2.0 * math.pi / size
    )
    squared = wave[:, None, None] ** 2 + wave[None, :, None] ** 2 + wave[None, None, :] ** 2
    return jnp.where(squared > 0, 1.0 / (squared + screening), 0.0)


def along(table, values, axis):
    forms = {1: "kn,cnyz->ckyz", 2: "kn,cxnz->cxkz", 3: "kn,cxyn->cxyk"}
    return jnp.einsum(forms[axis], table, values, precision=lax.Precision.HIGHEST)


def screened_solve(field):
    size = field.shape[1]
    index = jnp.arange(size, dtype=jnp.int32)
    phase = index[:, None] * index[None, :] % size
    angle = phase.astype(jnp.float32) * (2.0 * math.pi / size)
    cos_table = jnp.cos(angle)
    sin_table = jnp.sin(angle)
    real_part = along(cos_table, field, 3)
    imag_part = -along(sin_table, field, 3)
    for axis in (2, 1):
        real_part, imag_part = (
            along(cos_table, real_part, axis) + along(sin_table, imag_part, axis),
            along(cos_table, imag_part, axis) - along(sin_table, real_part, axis),
        )
    weights = kernel_table(size)
    real_part = real_part * weights
    imag_part = imag_part * weights
    for axis in (1, 2):
        real_part, imag_part = (
            along(cos_table, real_part, axis) - along(sin_table, imag_part, axis),
            along(cos_table, imag_part, axis) + along(sin_table, real_part, axis),
        )
    result = along(cos_table, real_part, 3) - along(sin_table, imag_part, 3)
    return result / float(size**3)


def local_columns(orbitals, points, cinv):
    ranks = lax.axis_size(("grid", "col"))
    local_rows = orbitals.shape[0]
    orbital_count = orbitals.shape[1]
    npoints = cinv.shape[0]
    columns = cinv.shape[1]
    per_rank = columns // ranks
    first_row = lax.axis_index(("grid", "col")) * local_rows
    offset = points - first_row
    inside = (offset >= 0) & (offset < local_rows)
    picked = jnp.take(orbitals, jnp.clip(offset, 0, local_rows - 1), axis=0)
    picked = jnp.where(inside[:, None], picked.astype(jnp.float32), 0.0)
    point_rows = lax.psum(picked, ("grid", "col")).astype(jnp.bfloat16)
    scale = 1.0 / math.sqrt(orbital_count)
    block_rows = math.gcd(local_rows, 1152)

    def pair_block(block):
        product = (
            lax.dot_general(
                block, point_rows, (((1,), (1,)), ((), ())), preferred_element_type=jnp.float32
            )
            * scale
        )
        return (product * product).astype(jnp.bfloat16)

    pairs = lax.map(
        pair_block, orbitals.reshape(local_rows // block_rows, block_rows, orbital_count)
    )
    pairs = pairs.reshape(local_rows, npoints)
    theta_cols = lax.dot_general(
        cinv, pairs, (((0,), (1,)), ((), ())), preferred_element_type=jnp.float32
    )
    fields = lax.all_to_all(theta_cols, ("grid", "col"), split_axis=0, concat_axis=1, tiled=True)
    fields = fields.reshape(per_rank, NX, NX, NX)
    potentials = screened_solve(fields).astype(jnp.bfloat16).reshape(per_rank, NX * NX * NX)
    rows_back = lax.all_to_all(potentials, ("grid", "col"), split_axis=1, concat_axis=0, tiled=True)
    factor = math.sqrt(npoints) / float(NX**3)
    halfway = lax.psum_scatter(
        lax.dot_general(
            pairs, rows_back, (((0,), (1,)), ((), ())), preferred_element_type=jnp.float32
        )
        * factor,
        "grid",
        scatter_dimension=0,
        tiled=True,
    )
    coupling = lax.psum_scatter(halfway, "col", scatter_dimension=0, tiled=True)
    return (rows_back, coupling)


AXES = ("grid", "col")
BF16, F32 = jnp.bfloat16, jnp.float32


def basis(size):
    wave = np.arange(size)[:, None]
    cell = np.arange(size)[None, :]
    angle = 2.0 * np.pi * (wave * cell % size) / size
    rows = np.where(2 * wave <= size, np.cos(angle), np.sin(angle)) * np.sqrt(2.0 / size)
    rows[0] = np.sqrt(1.0 / size)
    if size % 2 == 0:
        rows[size // 2] *= np.sqrt(0.5)
    number = np.minimum(np.arange(size), size - np.arange(size))
    return rows, (number * (2.0 * np.pi / size)) ** 2


def split_tables(table):
    high = np.asarray(table, BF16)
    low = np.asarray(table - high.astype(np.float64), BF16)
    both = np.concatenate([high, low], axis=1)
    return jnp.asarray(both), jnp.asarray(np.concatenate([both, high], axis=1))


def dot(left, right):
    return lax.dot_general(left, right, (((1,), (0,)), ((), ())), preferred_element_type=F32)


def apply_exact(table, values):
    return dot(table, jnp.concatenate([values, values], axis=0))


def apply_split(table, values):
    high = values.astype(BF16)
    low = (values - high.astype(F32)).astype(BF16)
    return dot(table, jnp.concatenate([high, high, low], axis=0))


LANES = 128
UNROLL = 2
BLOCK = 256


def across(ref, index, size):
    rows = pl.ds(index, size, stride=size + 1)
    return jnp.concatenate([ref[half, rows, :] for half in range(ref.shape[0])], axis=1)


def put_line(ref, line, size, value):
    rows = pl.ds(line * (size + 1), size)
    for half in range(ref.shape[0]):
        ref[half, rows, :] = value[:, half * LANES : (half + 1) * LANES]


def fit_kernel(size, scale, single, orb_ref, pts_ref, cinv_ref, table_ref, *rest):
    if not single:
        rest = rest[1:]
    pair_ref, outs, (field, points, shift, theta) = rest[0], rest[1:-4], rest[-4:]
    plane, step = pl.program_id(0), pl.program_id(1)
    rows = orb_ref.shape[0]
    npoints = pts_ref.shape[0]
    thirds = outs[0].shape[1] + (0 if single else 1)
    table = table_ref[...]

    @pl.when((plane == 0) & (step == 0))
    def _():
        scaled = pts_ref[...].astype(F32) * scale
        points[...] = scaled.astype(BF16)
        square = scaled * scaled
        norm = jnp.sum(square, axis=1, keepdims=True)
        mean = norm * (jnp.sum(norm) / npoints)
        shift[...] = jnp.sum(mean * cinv_ref[...].astype(F32), axis=0, keepdims=True)

    for start in range(0, npoints, BLOCK):
        part = slice(start, start + BLOCK)
        product = lax.dot_general(
            orb_ref[...], points[part], (((1,), (1,)), ((), ())), preferred_element_type=F32
        )
        pair_ref[:, part] = (product * product).astype(BF16)
    theta[...] = dot(pair_ref[...], cinv_ref[...]) - shift[...]
    for line in range(rows // size):
        value = apply_split(table, theta[line * size : (line + 1) * size])
        put_line(field, step * (rows // size) + line, size, value)

    @pl.when(step == pl.num_programs(1) - 1)
    def _():
        def body(owner, carry):
            for third in range(thirds):
                value = across(field, owner * thirds + third, size)
                value = apply_split(table, value).astype(BF16)
                if single:
                    outs[0][owner, third] = value
                elif third < thirds - 1:
                    outs[0][owner, third, plane] = value
                else:
                    outs[1][owner, plane] = value
            return carry

        lax.fori_loop(0, size // thirds, body, 0, unroll=UNROLL)


def solve_kernel(size, start, passed, wave_b_ref, wave_c_ref, wave_a_ref, table_ref, back_ref, *rest):
    first_ref, rest_ref = rest[:2]
    most_ref, last_ref, field, solved = rest[2 + passed :]
    whole = start > 0
    owners, later = rest_ref.shape[0], rest_ref.shape[1 if whole else 2]
    wave_c = wave_c_ref[start + pl.program_id(0)]

    def widen(owner, carry):
        for plane in range(later + 1):
            if plane == 0:
                value = first_ref[owner, 0]
            else:
                value = rest_ref[owner, plane - 1] if whole else rest_ref[owner, 0, plane - 1]
            put_line(field, plane * owners + owner, size, value.astype(F32))
        return carry

    lax.fori_loop(0, owners, widen, 0)
    table, back = table_ref[...], back_ref[...]
    wave_a = wave_a_ref[...]

    def body(mode, carry):
        value = apply_exact(table, across(field, mode, size).astype(BF16))
        squared = wave_a + (wave_b_ref[mode] + wave_c)
        weight = jnp.where(squared > 0, 1.0 / (squared + screening), 0.0)
        put_line(solved, mode, size, apply_split(back, value * weight))
        return carry

    lax.fori_loop(0, size, body, 0, unroll=UNROLL)

    def narrow(owner, carry):
        for plane in range(later + 1):
            value = across(solved, plane * owners + owner, size).astype(BF16)
            if plane == later:
                last_ref[owner, 0] = value
            elif whole:
                most_ref[owner, plane] = value
            else:
                most_ref[owner, 0, plane] = value
        return carry

    lax.fori_loop(0, owners, narrow, 0)


def couple_kernel(size, first, last, factor, *rest):
    count = 1 if last else 2
    sources, (exact_ref, table_ref, pair_ref) = rest[:count], rest[count : count + 3]
    rest = rest[count + 3 :]
    if not first:
        before_ref, rest = rest[0], rest[2:]
    out_ref, total_ref, field, block, total = rest
    step = pl.program_id(0)
    table = table_ref[...]
    rows = pair_ref.shape[0]
    owners = sources[0].shape[0]
    thirds = size // owners

    @pl.when(step == 0)
    def _():
        if first:
            total[...] = jnp.zeros_like(total)
        else:
            total[...] = before_ref[...]

        def body(owner, carry):
            for third in range(thirds):
                if last:
                    value = sources[0][owner, third]
                elif third < thirds - 1:
                    value = sources[0][owner, third, 0]
                else:
                    value = sources[1][owner, 0]
                value = apply_exact(exact_ref[...], value)
                put_line(field, owner * thirds + third, size, value)
            return carry

        lax.fori_loop(0, owners, body, 0, unroll=UNROLL)

    for line in range(rows // size):
        value = across(field, step * (rows // size) + line, size)
        block[line * size : (line + 1) * size, :] = apply_split(table, value)
    turned = block[...].T.astype(BF16)
    out_ref[...] = turned
    total[...] += dot(turned, pair_ref[...])

    @pl.when(step == pl.num_programs(0) - 1)
    def _():
        if last:
            total_ref[...] = total[...].T * factor
        else:
            total_ref[...] = total[...]


def const_spec(shape):
    return pl.BlockSpec(shape, lambda *_: (0,) * len(shape))


def cost(flops, moved):
    return pl.CostEstimate(flops=int(flops), bytes_accessed=int(moved), transcendentals=0)


VMEM = 65472 * 1024


def row_blocks(size, lines):
    while size % lines:
        lines -= 1
    return lines * size, size // lines


def local_planes(orbitals, points, cinv):
    size = NX
    ranks = lax.axis_size(AXES)
    rank = lax.axis_index(AXES)
    local_rows, orbital_count = orbitals.shape
    npoints, columns = cinv.shape
    plane_rows = size * size
    planes = local_rows // plane_rows
    later = planes - 1
    halves = columns // LANES

    arrivals = []

    def exchange(array):
        if arrivals:
            array, _ = lax.optimization_barrier((array, arrivals[-1]))
        arrivals.append(lax.all_to_all(array, AXES, 0, 0, tiled=True))
        return arrivals[-1]

    chips = lax.axis_size("grid")
    core = lax.axis_index("col")

    def swap(array):
        return lax.ppermute(array, "col", [(0, 1), (1, 0)])

    def scatter_sum(array):
        array = array.reshape(chips, 2, npoints // ranks, -1)
        own = lax.dynamic_index_in_dim(array, core, 1, keepdims=False)
        array = own + swap(lax.dynamic_index_in_dim(array, 1 - core, 1, keepdims=False))
        array = lax.all_to_all(array, "grid", 0, 0, tiled=True)
        return jnp.sum(array.astype(F32), axis=0).astype(array.dtype)

    offset = points - rank * local_rows
    inside = (offset >= 0) & (offset < local_rows)
    picked = jnp.take(orbitals, jnp.clip(offset, 0, local_rows - 1), axis=0)
    picked = jnp.where(inside[:, None], picked, jnp.zeros_like(picked))
    share = scatter_sum(picked)
    share = jnp.broadcast_to(share[None], (chips, *share.shape))
    own = lax.all_to_all(share, "grid", 0, 0, tiled=True)
    both = jnp.stack([own, swap(own)], axis=1)
    point_rows = jnp.where(core == 0, both, both[:, ::-1]).reshape(npoints, orbital_count)

    rows, squared = basis(size)
    _, forward = split_tables(rows)
    inverse_exact, inverse = split_tables(rows.T)
    order = (np.arange(ranks)[None, :] * planes + np.arange(planes)[:, None]).reshape(-1)
    forward_a, _ = split_tables(rows[:, order])
    _, inverse_a = split_tables(rows.T[order])
    wave = jnp.asarray(squared, F32)
    wave_a = jnp.asarray(np.broadcast_to(squared[:, None], (size, columns)), F32)

    block_rows, steps = row_blocks(size, 16)
    scale = 1.0 / math.sqrt(orbital_count)
    transform = 2 * 3 * plane_rows * size * columns
    tile = (size, columns)

    smem = pl.BlockSpec(memory_space=pltpu.SMEM)
    anywhere = pl.BlockSpec(memory_space=pl.ANY)

    def fit(start, count, *after):
        if count == 1 and start == 0:
            shapes = [(ranks, planes, *tile)]
        else:
            shapes = [(ranks, planes - 1, count, *tile), (ranks, count, *tile)]
        pair, *sent = pl.pallas_call(
            functools.partial(fit_kernel, size, scale, start == 0),
            grid=(count, steps),
            in_specs=[
                pl.BlockSpec((block_rows, orbital_count), lambda p, i: ((start + p) * steps + i, 0)),
                const_spec((npoints, orbital_count)),
                const_spec((npoints, columns)),
                const_spec(forward.shape),
            ]
            + [anywhere] * len(after),
            out_specs=[pl.BlockSpec((block_rows, npoints), lambda p, i: (p * steps + i, 0))]
            + [const_spec(shape) for shape in shapes],
            out_shape=[jax.ShapeDtypeStruct((count * plane_rows, npoints), BF16)]
            + [jax.ShapeDtypeStruct(shape, BF16) for shape in shapes],
            scratch_shapes=[
                pltpu.VMEM((halves, size * (size + 1), LANES), F32),
                pltpu.VMEM((npoints, orbital_count), BF16),
                pltpu.VMEM((1, columns), F32),
                pltpu.VMEM((block_rows, columns), F32),
            ],
            compiler_params=pltpu.CompilerParams(
                dimension_semantics=("arbitrary", "arbitrary"), vmem_limit_bytes=VMEM
            ),
            cost_estimate=cost(
                count * (2 * plane_rows * npoints * (orbital_count + columns) + 2 * transform),
                count * plane_rows * (2 * orbital_count + 2 * npoints + 2 * columns),
            ),
            name="fit",
        )(orbitals, point_rows, cinv, forward, *after)
        return pair, sent

    pair_first, (sent_first,) = fit(0, 1)
    arrived_first = exchange(sent_first)
    pair_rest, sent_rest = fit(1, later, pair_first)
    arrived_most, arrived_last = [exchange(value) for value in sent_rest]

    wave_c = lax.dynamic_slice(wave, (rank * planes,), (planes,))

    def solve(start, count, arrived, *passed):
        operands = [wave, wave_c, wave_a, forward_a, inverse_a, arrived_first, arrived, *passed]
        third_spec = pl.BlockSpec((ranks, 1, *tile), lambda i: (0, start + i, 0, 0))
        if start > 0:
            most_shape = (ranks, later, *tile)
            most_spec = const_spec(most_shape)
        else:
            most_shape = (ranks, count, later, *tile)
            most_spec = pl.BlockSpec((ranks, 1, later, *tile), lambda i: (0, i, 0, 0, 0))
        return pl.pallas_call(
            functools.partial(solve_kernel, size, start, len(passed)),
            grid=(count,),
            in_specs=[smem, smem]
            + [const_spec(value.shape) for value in operands[2:5]]
            + [third_spec, most_spec]
            + [anywhere] * len(passed),
            out_specs=[most_spec, third_spec],
            out_shape=[
                jax.ShapeDtypeStruct(most_shape, BF16),
                jax.ShapeDtypeStruct((ranks, planes, *tile), BF16),
            ],
            scratch_shapes=[pltpu.VMEM((halves, size * (size + 1), LANES), F32)] * 2,
            input_output_aliases={7: 1} if passed else {},
            compiler_params=pltpu.CompilerParams(
                dimension_semantics=("arbitrary",), vmem_limit_bytes=VMEM
            ),
            cost_estimate=cost(2 * count * transform, 4 * count * plane_rows * columns),
            name="solve",
        )(*operands)

    back_most, back_end = solve(0, later, arrived_most)
    arrived_most = exchange(back_most)
    back_last, back_end = solve(later, 1, arrived_last, back_end)
    arrived_last = exchange(back_last)
    arrived_end = exchange(back_end)

    factor = math.sqrt(npoints) / float(size**3)
    block_rows, steps = row_blocks(size, 8)
    potential = total = None
    for plane in range(planes):
        first, last = plane == 0, plane == planes - 1
        pair_start = 0 if first else (plane - 1) * steps
        if last:
            sources, in_specs = [arrived_end], [const_spec(arrived_end.shape)]
        else:
            sources = [arrived_most, arrived_last]
            in_specs = [
                pl.BlockSpec((ranks, later, 1, *tile), lambda i, plane=plane: (0, 0, plane, 0, 0)),
                pl.BlockSpec((ranks, 1, *tile), lambda i, plane=plane: (0, plane, 0, 0)),
            ]
        in_specs += [
            const_spec(inverse_exact.shape),
            const_spec(inverse.shape),
            pl.BlockSpec((block_rows, npoints), lambda i, start=pair_start: (start + i, 0)),
        ]
        operands = [*sources, inverse_exact, inverse, pair_first if first else pair_rest]
        if not first:
            in_specs += [const_spec(total.shape), anywhere]
            operands += [total, potential]
        total_shape = (npoints, columns) if last else (columns, npoints)
        potential, total = pl.pallas_call(
            functools.partial(couple_kernel, size, first, last, factor),
            grid=(steps,),
            in_specs=in_specs,
            out_specs=[
                pl.BlockSpec((columns, block_rows), lambda i, plane=plane: (0, plane * steps + i)),
                const_spec(total_shape),
            ],
            out_shape=[
                jax.ShapeDtypeStruct((columns, local_rows), BF16),
                jax.ShapeDtypeStruct(total_shape, F32),
            ],
            scratch_shapes=[
                pltpu.VMEM((halves, size * (size + 1), LANES), F32),
                pltpu.VMEM((block_rows, columns), F32),
                pltpu.VMEM((columns, npoints), F32),
            ],
            input_output_aliases={} if first else {len(operands) - 1: 0},
            compiler_params=pltpu.CompilerParams(
                dimension_semantics=("arbitrary",), vmem_limit_bytes=VMEM
            ),
            cost_estimate=cost(
                2 * plane_rows * npoints * columns + 2 * transform,
                plane_rows * (2 * npoints + 4 * columns),
            ),
            name="couple",
        )(*operands)

    return potential, scatter_sum(total)


def local(orbitals, points, cinv):
    size = NX
    ranks = lax.axis_size(AXES)
    rows, orbital_count = orbitals.shape
    npoints, columns = cinv.shape
    whole = rows * ranks == size**3 and rows % (size * size) == 0 and size % 16 == 0
    whole = whole and rows >= 2 * size * size and lax.axis_size("col") == 2
    exact = math.frexp(1.0 / math.sqrt(orbital_count))[0] == 0.5
    if whole and exact and columns % LANES == 0 and npoints % (ranks * 8) == 0:
        return local_planes(orbitals, points, cinv)
    return local_columns(orbitals, points, cinv)


def solution(mesh):
    in_specs = (P(("grid", "col"), None), P(), P())
    out_specs = (P(None, ("grid", "col")), P(("grid", "col"), None))
    return jax.shard_map(local, mesh=mesh, in_specs=in_specs, out_specs=out_specs, check_vma=False)
```

```python
import functools
import math

import jax
import jax.numpy as jnp
import numpy as np
from jax import lax
from jax.experimental import pallas as pl
from jax.experimental.pallas import tpu as pltpu
from jax.sharding import PartitionSpec as P


NX = 96


screening = 0.25


def kernel_table(size):
    index = jnp.arange(size)
    wave = jnp.where(index < (size + 1) // 2, index, index - size).astype(jnp.float32) * (
        2.0 * math.pi / size
    )
    squared = wave[:, None, None] ** 2 + wave[None, :, None] ** 2 + wave[None, None, :] ** 2
    return jnp.where(squared > 0, 1.0 / (squared + screening), 0.0)


def along(table, values, axis):
    forms = {1: "kn,cnyz->ckyz", 2: "kn,cxnz->cxkz", 3: "kn,cxyn->cxyk"}
    return jnp.einsum(forms[axis], table, values, precision=lax.Precision.HIGHEST)


def screened_solve(field):
    size = field.shape[1]
    index = jnp.arange(size, dtype=jnp.int32)
    phase = index[:, None] * index[None, :] % size
    angle = phase.astype(jnp.float32) * (2.0 * math.pi / size)
    cos_table = jnp.cos(angle)
    sin_table = jnp.sin(angle)
    real_part = along(cos_table, field, 3)
    imag_part = -along(sin_table, field, 3)
    for axis in (2, 1):
        real_part, imag_part = (
            along(cos_table, real_part, axis) + along(sin_table, imag_part, axis),
            along(cos_table, imag_part, axis) - along(sin_table, real_part, axis),
        )
    weights = kernel_table(size)
    real_part = real_part * weights
    imag_part = imag_part * weights
    for axis in (1, 2):
        real_part, imag_part = (
            along(cos_table, real_part, axis) - along(sin_table, imag_part, axis),
            along(cos_table, imag_part, axis) + along(sin_table, real_part, axis),
        )
    result = along(cos_table, real_part, 3) - along(sin_table, imag_part, 3)
    return result / float(size**3)


def local_columns(orbitals, points, cinv):
    ranks = lax.axis_size(("grid", "col"))
    local_rows = orbitals.shape[0]
    orbital_count = orbitals.shape[1]
    npoints = cinv.shape[0]
    columns = cinv.shape[1]
    per_rank = columns // ranks
    first_row = lax.axis_index(("grid", "col")) * local_rows
    offset = points - first_row
    inside = (offset >= 0) & (offset < local_rows)
    picked = jnp.take(orbitals, jnp.clip(offset, 0, local_rows - 1), axis=0)
    picked = jnp.where(inside[:, None], picked.astype(jnp.float32), 0.0)
    point_rows = lax.psum(picked, ("grid", "col")).astype(jnp.bfloat16)
    scale = 1.0 / math.sqrt(orbital_count)
    block_rows = math.gcd(local_rows, 1152)

    def pair_block(block):
        product = (
            lax.dot_general(
                block, point_rows, (((1,), (1,)), ((), ())), preferred_element_type=jnp.float32
            )
            * scale
        )
        return (product * product).astype(jnp.bfloat16)

    pairs = lax.map(
        pair_block, orbitals.reshape(local_rows // block_rows, block_rows, orbital_count)
    )
    pairs = pairs.reshape(local_rows, npoints)
    theta_cols = lax.dot_general(
        cinv, pairs, (((0,), (1,)), ((), ())), preferred_element_type=jnp.float32
    )
    fields = lax.all_to_all(theta_cols, ("grid", "col"), split_axis=0, concat_axis=1, tiled=True)
    fields = fields.reshape(per_rank, NX, NX, NX)
    potentials = screened_solve(fields).astype(jnp.bfloat16).reshape(per_rank, NX * NX * NX)
    rows_back = lax.all_to_all(potentials, ("grid", "col"), split_axis=1, concat_axis=0, tiled=True)
    factor = math.sqrt(npoints) / float(NX**3)
    halfway = lax.psum_scatter(
        lax.dot_general(
            pairs, rows_back, (((0,), (1,)), ((), ())), preferred_element_type=jnp.float32
        )
        * factor,
        "grid",
        scatter_dimension=0,
        tiled=True,
    )
    coupling = lax.psum_scatter(halfway, "col", scatter_dimension=0, tiled=True)
    return (rows_back, coupling)


AXES = ("grid", "col")
BF16, F32 = jnp.bfloat16, jnp.float32


def basis(size):
    wave = np.arange(size)[:, None]
    cell = np.arange(size)[None, :]
    angle = 2.0 * np.pi * (wave * cell % size) / size
    rows = np.where(2 * wave <= size, np.cos(angle), np.sin(angle)) * np.sqrt(2.0 / size)
    rows[0] = np.sqrt(1.0 / size)
    if size % 2 == 0:
        rows[size // 2] *= np.sqrt(0.5)
    number = np.minimum(np.arange(size), size - np.arange(size))
    return rows, (number * (2.0 * np.pi / size)) ** 2


def split_tables(table):
    high = np.asarray(table, BF16)
    low = np.asarray(table - high.astype(np.float64), BF16)
    both = np.concatenate([high, low], axis=1)
    return jnp.asarray(both), jnp.asarray(np.concatenate([both, high], axis=1))


def dot(left, right):
    return lax.dot_general(left, right, (((1,), (0,)), ((), ())), preferred_element_type=F32)


def apply_exact(table, values):
    return dot(table, jnp.concatenate([values, values], axis=0))


def apply_split(table, values):
    high = values.astype(BF16)
    low = (values - high.astype(F32)).astype(BF16)
    return dot(table, jnp.concatenate([high, high, low], axis=0))


LANES = 128
UNROLL = 2
BLOCK = 256


def across(ref, index, size):
    rows = pl.ds(index, size, stride=size + 1)
    return jnp.concatenate([ref[half, rows, :] for half in range(ref.shape[0])], axis=1)


def put_line(ref, line, size, value):
    rows = pl.ds(line * (size + 1), size)
    for half in range(ref.shape[0]):
        ref[half, rows, :] = value[:, half * LANES : (half + 1) * LANES]


def fit_kernel(size, scale, single, orb_ref, pts_ref, cinv_ref, table_ref, *rest):
    if not single:
        rest = rest[1:]
    pair_ref, outs, (field, points, shift, theta) = rest[0], rest[1:-4], rest[-4:]
    plane, step = pl.program_id(0), pl.program_id(1)
    rows = orb_ref.shape[0]
    npoints = pts_ref.shape[0]
    thirds = outs[0].shape[1] + (0 if single else 1)
    table = table_ref[...]

    @pl.when((plane == 0) & (step == 0))
    def _():
        scaled = pts_ref[...].astype(F32) * scale
        points[...] = scaled.astype(BF16)
        square = scaled * scaled
        norm = jnp.sum(square, axis=1, keepdims=True)
        mean = norm * (jnp.sum(norm) / npoints)
        shift[...] = jnp.sum(mean * cinv_ref[...].astype(F32), axis=0, keepdims=True)

    for start in range(0, npoints, BLOCK):
        part = slice(start, start + BLOCK)
        product = lax.dot_general(
            orb_ref[...], points[part], (((1,), (1,)), ((), ())), preferred_element_type=F32
        )
        pair_ref[:, part] = (product * product).astype(BF16)
    theta[...] = dot(pair_ref[...], cinv_ref[...]) - shift[...]
    for line in range(rows // size):
        value = apply_split(table, theta[line * size : (line + 1) * size])
        put_line(field, step * (rows // size) + line, size, value)

    @pl.when(step == pl.num_programs(1) - 1)
    def _():
        def body(owner, carry):
            for third in range(thirds):
                value = across(field, owner * thirds + third, size)
                value = apply_split(table, value).astype(BF16)
                if single:
                    outs[0][owner, third] = value
                elif third < thirds - 1:
                    outs[0][owner, third, plane] = value
                else:
                    outs[1][owner, plane] = value
            return carry

        lax.fori_loop(0, size // thirds, body, 0, unroll=UNROLL)


def solve_kernel(size, start, passed, wave_b_ref, wave_c_ref, wave_a_ref, table_ref, back_ref, *rest):
    first_ref, rest_ref = rest[:2]
    most_ref, last_ref, field, solved = rest[2 + passed :]
    whole = start > 0
    owners, later = rest_ref.shape[0], rest_ref.shape[1 if whole else 2]
    wave_c = wave_c_ref[start + pl.program_id(0)]

    def widen(owner, carry):
        for plane in range(later + 1):
            if plane == 0:
                value = first_ref[owner, 0]
            else:
                value = rest_ref[owner, plane - 1] if whole else rest_ref[owner, 0, plane - 1]
            put_line(field, plane * owners + owner, size, value.astype(F32))
        return carry

    lax.fori_loop(0, owners, widen, 0)
    table, back = table_ref[...], back_ref[...]
    wave_a = wave_a_ref[...]

    def body(mode, carry):
        value = apply_exact(table, across(field, mode, size).astype(BF16))
        squared = wave_a + (wave_b_ref[mode] + wave_c)
        weight = jnp.where(squared > 0, 1.0 / (squared + screening), 0.0)
        put_line(solved, mode, size, apply_split(back, value * weight))
        return carry

    lax.fori_loop(0, size, body, 0, unroll=UNROLL)

    def narrow(owner, carry):
        for plane in range(later + 1):
            value = across(solved, plane * owners + owner, size).astype(BF16)
            if plane == later:
                last_ref[owner, 0] = value
            elif whole:
                most_ref[owner, plane] = value
            else:
                most_ref[owner, 0, plane] = value
        return carry

    lax.fori_loop(0, owners, narrow, 0)


def couple_kernel(size, first, last, rows, *rest):
    count = 1 if last else 2
    sources, (exact_ref, table_ref, pair_ref) = rest[:count], rest[count : count + 3]
    rest = rest[count + 3 :]
    if last:
        out_ref, field, block = rest[2:]
    else:
        if not first:
            before_ref, rest = rest[0], rest[2:]
        out_ref, total_ref, field, block, total = rest
    step = pl.program_id(0)
    table = table_ref[...]
    owners = sources[0].shape[0]
    thirds = size // owners

    @pl.when(step == 0)
    def _():
        if first:
            total[...] = jnp.zeros_like(total)
        elif not last:
            total[...] = before_ref[...]

        def body(owner, carry):
            for third in range(thirds):
                if last:
                    value = sources[0][owner, third]
                elif third < thirds - 1:
                    value = sources[0][owner, third, 0]
                else:
                    value = sources[1][owner, 0]
                value = apply_exact(exact_ref[...], value)
                put_line(field, owner * thirds + third, size, value)
            return carry

        lax.fori_loop(0, owners, body, 0, unroll=UNROLL)

    for line in range(rows // size):
        value = across(field, step * (rows // size) + line, size)
        block[line * size : (line + 1) * size, :] = apply_split(table, value)
    turned = block[...].T.astype(BF16)
    out_ref[...] = turned
    if last:
        return
    total[...] += dot(turned, pair_ref[...])

    @pl.when(step == pl.num_programs(0) - 1)
    def _():
        total_ref[...] = total[...]


def spectrum_kernel(size, exact_ref, table_ref, pair_ref, out_ref, low_ref, field, block):
    step = pl.program_id(1)
    rows = pair_ref.shape[0]
    lines = block.shape[0] // size
    for line in range(rows // size):
        value = apply_exact(exact_ref[...], pair_ref[line * size : (line + 1) * size, :])
        put_line(field, step * (rows // size) + line, size, value)

    @pl.when(step == pl.num_programs(1) - 1)
    def _():
        value = apply_split(table_ref[...], across(field, 0, size))
        low_ref[...] = (value - value.astype(BF16).astype(F32)).astype(BF16)

        def body(group, carry):
            for line in range(lines):
                value = apply_split(table_ref[...], across(field, group * lines + line, size))
                block[line * size : (line + 1) * size, :] = value.astype(BF16)
            start = pl.multiple_of(group * lines * size, lines * size)
            out_ref[:, pl.ds(start, lines * size)] = block[...].T
            return carry

        lax.fori_loop(0, size // lines, body, 0)


def contract_kernel(size, factor, before_ref, low_ref, left_ref, right_ref, out_ref):
    step = pl.program_id(0)

    @pl.when(step == 0)
    def _():
        low = lax.dot_general(
            low_ref[...], right_ref[:size, :], (((0,), (0,)), ((), ())), preferred_element_type=F32
        )
        out_ref[...] = before_ref[...].T + low

    out_ref[...] += dot(left_ref[...], right_ref[...])

    @pl.when(step == pl.num_programs(0) - 1)
    def _():
        out_ref[...] = out_ref[...] * factor


def const_spec(shape):
    return pl.BlockSpec(shape, lambda *_: (0,) * len(shape))


def cost(flops, moved):
    return pl.CostEstimate(flops=int(flops), bytes_accessed=int(moved), transcendentals=0)


VMEM = 65472 * 1024


def row_blocks(size, lines):
    while size % lines:
        lines -= 1
    return lines * size, size // lines


def local_planes(orbitals, points, cinv):
    size = NX
    ranks = lax.axis_size(AXES)
    rank = lax.axis_index(AXES)
    local_rows, orbital_count = orbitals.shape
    npoints, columns = cinv.shape
    plane_rows = size * size
    planes = local_rows // plane_rows
    later = planes - 1
    halves = columns // LANES

    arrivals = []

    def exchange(array):
        if arrivals:
            array, _ = lax.optimization_barrier((array, arrivals[-1]))
        arrivals.append(lax.all_to_all(array, AXES, 0, 0, tiled=True))
        return arrivals[-1]

    chips = lax.axis_size("grid")
    core = lax.axis_index("col")

    def swap(array):
        return lax.ppermute(array, "col", [(0, 1), (1, 0)])

    def pair_sum(array):
        array = array.reshape(chips, 2, npoints // ranks, -1)
        own = lax.dynamic_index_in_dim(array, core, 1, keepdims=False)
        return own + swap(lax.dynamic_index_in_dim(array, 1 - core, 1, keepdims=False))

    offset = points - rank * local_rows
    inside = (offset >= 0) & (offset < local_rows)
    picked = jnp.take(orbitals, jnp.clip(offset, 0, local_rows - 1), axis=0)
    picked = jnp.where(inside[:, None], picked, jnp.zeros_like(picked))
    shares = lax.all_to_all(pair_sum(picked), "grid", 0, 0, tiled=True)
    share = jnp.sum(shares.astype(F32), axis=0).astype(BF16)
    share = jnp.broadcast_to(share[None], (chips, *share.shape))
    own = lax.all_to_all(share, "grid", 0, 0, tiled=True)
    both = jnp.stack([own, swap(own)], axis=1)
    point_rows = jnp.where(core == 0, both, both[:, ::-1]).reshape(npoints, orbital_count)

    rows, squared = basis(size)
    forward_exact, forward = split_tables(rows)
    inverse_exact, inverse = split_tables(rows.T)
    order = (np.arange(ranks)[None, :] * planes + np.arange(planes)[:, None]).reshape(-1)
    forward_a, _ = split_tables(rows[:, order])
    _, inverse_a = split_tables(rows.T[order])
    wave = jnp.asarray(squared, F32)
    wave_a = jnp.asarray(np.broadcast_to(squared[:, None], (size, columns)), F32)

    block_rows, steps = row_blocks(size, 16)
    scale = 1.0 / math.sqrt(orbital_count)
    transform = 2 * 3 * plane_rows * size * columns
    tile = (size, columns)

    smem = pl.BlockSpec(memory_space=pltpu.SMEM)
    anywhere = pl.BlockSpec(memory_space=pl.ANY)

    def fit(start, count, *after):
        if count == 1 and start == 0:
            shapes = [(ranks, planes, *tile)]
        else:
            shapes = [(ranks, planes - 1, count, *tile), (ranks, count, *tile)]
        pair, *sent = pl.pallas_call(
            functools.partial(fit_kernel, size, scale, start == 0),
            grid=(count, steps),
            in_specs=[
                pl.BlockSpec((block_rows, orbital_count), lambda p, i: ((start + p) * steps + i, 0)),
                const_spec((npoints, orbital_count)),
                const_spec((npoints, columns)),
                const_spec(forward.shape),
            ]
            + [anywhere] * len(after),
            out_specs=[pl.BlockSpec((block_rows, npoints), lambda p, i: (p * steps + i, 0))]
            + [const_spec(shape) for shape in shapes],
            out_shape=[jax.ShapeDtypeStruct((count * plane_rows, npoints), BF16)]
            + [jax.ShapeDtypeStruct(shape, BF16) for shape in shapes],
            scratch_shapes=[
                pltpu.VMEM((halves, size * (size + 1), LANES), F32),
                pltpu.VMEM((npoints, orbital_count), BF16),
                pltpu.VMEM((1, columns), F32),
                pltpu.VMEM((block_rows, columns), F32),
            ],
            compiler_params=pltpu.CompilerParams(
                dimension_semantics=("arbitrary", "arbitrary"), vmem_limit_bytes=VMEM
            ),
            cost_estimate=cost(
                count * (2 * plane_rows * npoints * (orbital_count + columns) + 2 * transform),
                count * plane_rows * (2 * orbital_count + 2 * npoints + 2 * columns),
            ),
            name="fit",
        )(orbitals, point_rows, cinv, forward, *after)
        return pair, sent

    pair_first, (sent_first,) = fit(0, 1)
    arrived_first = exchange(sent_first)
    pair_rest, sent_rest = fit(1, later, pair_first)
    arrived_most, arrived_last = [exchange(value) for value in sent_rest]

    wave_c = lax.dynamic_slice(wave, (rank * planes,), (planes,))

    def solve(start, count, arrived, *passed):
        operands = [wave, wave_c, wave_a, forward_a, inverse_a, arrived_first, arrived, *passed]
        third_spec = pl.BlockSpec((ranks, 1, *tile), lambda i: (0, start + i, 0, 0))
        if start > 0:
            most_shape = (ranks, later, *tile)
            most_spec = const_spec(most_shape)
        else:
            most_shape = (ranks, count, later, *tile)
            most_spec = pl.BlockSpec((ranks, 1, later, *tile), lambda i: (0, i, 0, 0, 0))
        return pl.pallas_call(
            functools.partial(solve_kernel, size, start, len(passed)),
            grid=(count,),
            in_specs=[smem, smem]
            + [const_spec(value.shape) for value in operands[2:5]]
            + [third_spec, most_spec]
            + [anywhere] * len(passed),
            out_specs=[most_spec, third_spec],
            out_shape=[
                jax.ShapeDtypeStruct(most_shape, BF16),
                jax.ShapeDtypeStruct((ranks, planes, *tile), BF16),
            ],
            scratch_shapes=[pltpu.VMEM((halves, size * (size + 1), LANES), F32)] * 2,
            input_output_aliases={7: 1} if passed else {},
            compiler_params=pltpu.CompilerParams(
                dimension_semantics=("arbitrary",), vmem_limit_bytes=VMEM
            ),
            cost_estimate=cost(2 * count * transform, 4 * count * plane_rows * columns),
            name="solve",
        )(*operands)

    back_most, back_end = solve(0, later, arrived_most)
    arrived_most = exchange(back_most)
    back_last, back_end = solve(later, 1, arrived_last, back_end)
    block_rows, steps = row_blocks(size, 8)
    params = pltpu.CompilerParams(dimension_semantics=("arbitrary",), vmem_limit_bytes=VMEM)
    field = pltpu.VMEM((halves, size * (size + 1), LANES), F32)
    last_start = (later - 1) * steps
    modes, low = pl.pallas_call(
        functools.partial(spectrum_kernel, size),
        grid=(npoints // columns, steps),
        in_specs=[
            const_spec(forward_exact.shape),
            const_spec(forward.shape),
            pl.BlockSpec((block_rows, columns), lambda g, i: (last_start + i, g)),
        ],
        out_specs=[
            pl.BlockSpec((columns, plane_rows), lambda g, i: (g, 0)),
            pl.BlockSpec((size, columns), lambda g, i: (0, g)),
        ],
        out_shape=[
            jax.ShapeDtypeStruct((npoints, plane_rows), BF16),
            jax.ShapeDtypeStruct((size, npoints), BF16),
        ],
        scratch_shapes=[field, pltpu.VMEM((4 * size, columns), BF16)],
        compiler_params=pltpu.CompilerParams(
            dimension_semantics=("arbitrary", "arbitrary"), vmem_limit_bytes=VMEM
        ),
        cost_estimate=cost(
            2 * transform * npoints // columns, 4 * plane_rows * npoints
        ),
        name="spectrum",
    )(forward_exact, forward, pair_rest)
    back_last, modes, low = lax.optimization_barrier((back_last, modes, low))
    arrived_last = exchange(back_last)
    arrived_end = exchange(back_end)

    factor = math.sqrt(npoints) / float(size**3)
    potential = total = None
    for plane in range(planes):
        first, last = plane == 0, plane == planes - 1
        pair_start = 0 if first else (plane - 1) * steps
        if last:
            sources, in_specs = [arrived_end], [const_spec(arrived_end.shape)]
        else:
            sources = [arrived_most, arrived_last]
            in_specs = [
                pl.BlockSpec((ranks, later, 1, *tile), lambda i, plane=plane: (0, 0, plane, 0, 0)),
                pl.BlockSpec((ranks, 1, *tile), lambda i, plane=plane: (0, plane, 0, 0)),
            ]
        in_specs += [
            const_spec(inverse_exact.shape),
            const_spec(inverse.shape),
            pl.BlockSpec((block_rows, npoints), lambda i, start=pair_start: (start + i, 0)),
        ]
        operands = [*sources, inverse_exact, inverse, pair_first if first else pair_rest]
        if last:
            total = pl.pallas_call(
                functools.partial(contract_kernel, size, factor),
                grid=(steps,),
                in_specs=[
                    const_spec(total.shape),
                    const_spec(low.shape),
                    pl.BlockSpec((npoints, block_rows), lambda i: (0, i)),
                    pl.BlockSpec((block_rows, columns), lambda i: (i, 0)),
                ],
                out_specs=const_spec((npoints, columns)),
                out_shape=jax.ShapeDtypeStruct((npoints, columns), F32),
                compiler_params=params,
                cost_estimate=cost(
                    2 * plane_rows * npoints * columns, 2 * plane_rows * (npoints + columns)
                ),
                name="contract",
            )(total, low, modes, arrived_end.reshape(plane_rows, columns))
            total = pair_sum(total)
            operands[-1] = jnp.zeros((16, LANES), BF16)
            in_specs[-1] = const_spec((16, LANES))
            in_specs += [anywhere, anywhere]
            operands += [total, potential]
        elif not first:
            in_specs += [const_spec(total.shape), anywhere]
            operands += [total, potential]
        call = pl.pallas_call(
            functools.partial(couple_kernel, size, first, last, block_rows),
            grid=(steps,),
            in_specs=in_specs,
            out_specs=[
                pl.BlockSpec((columns, block_rows), lambda i, plane=plane: (0, plane * steps + i)),
                const_spec((columns, npoints)),
            ][: 1 if last else 2],
            out_shape=[
                jax.ShapeDtypeStruct((columns, local_rows), BF16),
                jax.ShapeDtypeStruct((columns, npoints), F32),
            ][: 1 if last else 2],
            scratch_shapes=[
                field,
                pltpu.VMEM((block_rows, columns), F32),
                pltpu.VMEM((columns, npoints), F32),
            ][: 2 if last else 3],
            input_output_aliases={} if first else {len(operands) - 1: 0},
            compiler_params=params,
            cost_estimate=cost(
                2 * plane_rows * npoints * columns + 2 * transform,
                plane_rows * (2 * npoints + 4 * columns),
            ),
            name="couple",
        )
        if last:
            (potential,) = call(*operands)
        else:
            potential, total = call(*operands)

    shares = lax.all_to_all(total, "grid", 0, 0, tiled=True)
    return potential, jnp.sum(shares, axis=0)


def local(orbitals, points, cinv):
    size = NX
    ranks = lax.axis_size(AXES)
    rows, orbital_count = orbitals.shape
    npoints, columns = cinv.shape
    whole = rows * ranks == size**3 and rows % (size * size) == 0 and size % 16 == 0
    whole = whole and rows >= 2 * size * size and lax.axis_size("col") == 2
    exact = math.frexp(1.0 / math.sqrt(orbital_count))[0] == 0.5
    if whole and exact and columns % LANES == 0 and npoints % (ranks * 8) == 0:
        return local_planes(orbitals, points, cinv)
    return local_columns(orbitals, points, cinv)


def solution(mesh):
    in_specs = (P(("grid", "col"), None), P(), P())
    out_specs = (P(None, ("grid", "col")), P(("grid", "col"), None))
    return jax.shard_map(
        local, mesh=mesh, in_specs=in_specs, out_specs=out_specs, check_vma=False
    )
```
